32 devices in a mesh: grp: 2 (over x), ctg: 16 (over z, y, core).
Axes of the slice: x: 2, y: 2, z: 4, core: 2. Of those that a mesh axis runs over, the one named last changes fastest.
Arguments:
- flow_tiles: bfloat16 [128, 256, 3072], P('ctg'), may hold values from -0.109375 to 0.109375
- tile_pattern: int32 [128, 2, 24], P('ctg'), may hold values 0 or 1
- monitored: int32 [128, 256], P('ctg'), may hold values from 0 to 16383
- ratings: float32 [16384], replicated, may hold values from 0.3 to 3
- base_flow: float32 [64, 128, 256], P('grp', 'ctg'), parts along dimension 0, may hold values from -6 to 6
- unit_cost: float32 [64, 3072], P(('grp', 'ctg')), parts along dimension 0, may hold values from -6 to 6
- unit_floor: float32 [3072], replicated, may hold values from 0 to 0.5
- unit_span: float32 [3072], replicated, may hold values from 0.5 to 2
- ramp_limit: float32 [3072], replicated, may hold values from 0.05 to 0.5
- ramp_mask: int32 [3072], replicated, may hold values 0 or 1
- demand: float32 [64], P(('grp', 'ctg')), parts along dimension 0, may hold values from 1228.8 to 2457.6
- start_output: float32 [64, 3072], P(('grp', 'ctg')), parts along dimension 0, may hold values from 0 to 1.5
- start_flow_dual: float32 [64, 128, 256], P('grp', 'ctg'), parts along dimension 0, may hold values from -2 to 2
- start_ramp_dual: float32 [64, 3072], P(('grp', 'ctg')), parts along dimension 0, may hold values from -3 to 3
Outputs:
- output_levels: float32 [64, 3072], P(('grp', 'ctg')), parts along dimension 0
- flow_dual: float32 [64, 128, 256], P('grp', 'ctg'), parts along dimension 0
- ramp_dual: float32 [64, 3072], P(('grp', 'ctg')), parts along dimension 0
- balance_price: float32 [64], P(('grp', 'ctg')), parts along dimension 0
The draws below stay inside these ranges and needn't reach their ends.
There are 2 independent parts, one for each index of `grp`. The reference program is written for one: setup_inputs(seed, part) draws one part's arguments, and reference() takes and returns one part's arrays. A program takes and returns all parts, laid end to end along the dimension named above; an argument that names none is the same for every part. Nothing has to cross between parts.
All inputs are finite; a program needn't handle non-finite values. No bound on the sum of `tile_pattern` on one device may be relied on, other than what follows from the above.
Results may differ from the reference program's by a relative error of at most 0.0045.
Values may be sent and summed in bfloat16 or wider, within the bound.
A program may use at most 128 MiB of HBM per device.

```python
import math
import jax
import jax.numpy as jnp
from jax import lax

UNITS = 3072
MON = 256
LINES = 16384
ITERS = 4
CTGS = 128
HOURS = 32


def draw_base_flow(key, part):
    severity = 0.5 + jnp.arange(CTGS, dtype=jnp.float32) / CTGS
    values = jnp.clip(jax.random.normal(key, (HOURS, CTGS, MON), jnp.float32), -4.0, 4.0)
    return values * severity[None, :, None]


def set_ends(result, own_key, smallest, high):
    longest = result.shape.index(max(result.shape))
    spots = []
    for shift in (0, 1):
        where = [jax.random.randint(jax.random.fold_in(own_key, axis), (), 0, length) for axis, length in enumerate(result.shape)]
        where[longest] = (where[longest] + shift) % result.shape[longest]
        spots.append(tuple(where))
    return result.at[spots[0]].set(smallest).at[spots[1]].set(high)


def shard_levels(key, dims, shards, smallest, high):
    gain = 1.0
    for dim, shards_of in shards:
        draws = jax.random.uniform(jax.random.fold_in(jax.random.fold_in(key, 6), dim), (shards_of,), jnp.float32, smallest / len(shards), high / len(shards))
        gain = gain * jnp.repeat(jnp.exp(draws), dims[dim] // shards_of).reshape((-1,) + (1,) * (len(dims) - 1 - dim))
    return gain


def centred(key, dims, width, limit, pieces=(), held_as=jnp.bfloat16):
    level = shard_levels(key, dims, pieces, -0.22, 0.18) if pieces else 1.0
    drawn = jax.random.normal(key, dims, jnp.float32) * width * level
    return jnp.minimum(jnp.maximum(drawn, -limit), limit).astype(held_as)


def setup_inputs(seed: int = 0, part: int = 0) -> dict:
    splits = jax.random.split(jax.random.key(seed), 15)
    part_splits = jax.random.split(jax.random.fold_in(splits[14], part), 15)
    flow_tiles = centred(splits[0], (CTGS, MON, UNITS), UNITS ** -0.5, 0.109375, ((0, 16),))
    tile_pattern = set_ends((jax.random.randint(splits[1], (CTGS, MON // 128, UNITS // 128), 0, 2) < 1).astype(jnp.int32), jax.random.fold_in(splits[1], 1), 0, 1)
    monitored = set_ends(jax.random.randint(splits[2], (CTGS, MON), 0, LINES), jax.random.fold_in(splits[2], 1), 0, LINES - 1).astype(jnp.int32)
    ratings = jnp.clip(jnp.exp(jax.random.uniform(splits[3], (LINES,), jnp.float32, math.log(0.3), math.log(3.0))), 0.3, 3.0)
    base_flow = draw_base_flow(jax.random.fold_in(jax.random.fold_in(splits[14], part), 71), part)
    unit_cost = centred(part_splits[5], (HOURS, UNITS), 1.0, 6.0, ((0, 16),), jnp.float32)
    unit_floor = jnp.clip(jax.random.uniform(splits[6], (UNITS,), jnp.float32, 0.0, 0.5), 0.0, 0.5)
    unit_span = jnp.clip(jnp.exp(jax.random.uniform(splits[7], (UNITS,), jnp.float32, math.log(0.5), math.log(2.0))), 0.5, 2.0)
    ramp_limit = jnp.clip(jnp.exp(jax.random.uniform(splits[8], (UNITS,), jnp.float32, math.log(0.05), math.log(0.5))), 0.05, 0.5)
    ramp_mask = set_ends((jax.random.randint(splits[9], (UNITS,), 0, 4) < 3).astype(jnp.int32), jax.random.fold_in(splits[9], 1), 0, 1)
    demand = jnp.clip(1228.8 + 1228.8 * jax.random.uniform(part_splits[10], (HOURS,), jnp.float32) ** shard_levels(part_splits[10], (HOURS,), ((0, 16),), -0.2, 0.2), 1228.8, 2457.6)
    start_output = jnp.clip(1.5 * jax.random.uniform(part_splits[11], (HOURS, UNITS), jnp.float32) ** shard_levels(part_splits[11], (HOURS, UNITS), ((0, 16),), -0.2, 0.2), 0.0, 1.5)
    start_flow_dual = centred(part_splits[12], (HOURS, CTGS, MON), 0.3, 2.0, ((1, 16),), jnp.float32)
    start_ramp_dual = centred(part_splits[13], (HOURS, UNITS), 0.5, 3.0, ((0, 16),), jnp.float32)
    return {"flow_tiles": flow_tiles, "tile_pattern": tile_pattern, "monitored": monitored, "ratings": ratings, "base_flow": base_flow, "unit_cost": unit_cost, "unit_floor": unit_floor, "unit_span": unit_span, "ramp_limit": ramp_limit, "ramp_mask": ramp_mask, "demand": demand, "start_output": start_output, "start_flow_dual": start_flow_dual, "start_ramp_dual": start_ramp_dual}


def mask_tiles(flow_tiles, tile_pattern):
    ctg_count, line_count, unit_count = flow_tiles.shape
    blocks = flow_tiles.reshape(ctg_count, line_count // 128, 128, unit_count // 128, 128)
    gates = tile_pattern.astype(jnp.bfloat16)[:, :, None, :, None]
    return (blocks * gates).reshape(ctg_count, line_count, unit_count)

def reference(flow_tiles, tile_pattern, monitored, ratings, base_flow, unit_cost, unit_floor, unit_span, ramp_limit, ramp_mask, demand, start_output, start_flow_dual, start_ramp_dual):
    masked = mask_tiles(flow_tiles, tile_pattern).astype(jnp.float32)
    flow_limit = ratings[monitored]
    flow_lower = base_flow - flow_limit[None]
    flow_upper = base_flow + flow_limit[None]
    step_size = 0.5 / (2.0 + math.sqrt(CTGS * MON / UNITS))
    balance = 1.0 / math.sqrt(UNITS)
    ceiling = unit_floor + unit_span
    ramp_on = ramp_mask.astype(jnp.float32)
    weight = jnp.float32(1.0)
    levels = start_output
    flow_dual = start_flow_dual
    ramp_dual = start_ramp_dual
    balance_price = jnp.zeros((HOURS,), jnp.float32)
    zero_row = jnp.zeros((1, UNITS), jnp.float32)
    for iteration in range(ITERS):
        primal_step = step_size / weight
        dual_step = step_size * weight
        dual_half = lax.optimization_barrier(flow_dual.astype(jnp.bfloat16)).astype(jnp.float32)
        pulled = jnp.einsum('tkm,kmu->tu', dual_half, masked, precision=lax.Precision.HIGHEST)
        before = jnp.concatenate([zero_row, ramp_dual[:-1]], axis=0)
        gradient = unit_cost + pulled + ramp_on * (before - ramp_dual) + balance * balance_price[:, None]
        moved = jnp.clip(levels - primal_step * gradient, unit_floor, ceiling)
        extended = 2.0 * moved - levels
        extended_half = lax.optimization_barrier(extended.astype(jnp.bfloat16)).astype(jnp.float32)
        flows = jnp.einsum('kmu,tu->tkm', masked, extended_half, precision=lax.Precision.HIGHEST)
        trial = flow_dual + dual_step * flows
        dual_new = trial - dual_step * jnp.clip(trial / dual_step, flow_lower, flow_upper)
        change = ramp_on * jnp.concatenate([extended[1:] - extended[:-1], zero_row], axis=0)
        ramp_trial = ramp_dual + dual_step * change
        ramp_new = ramp_trial - dual_step * jnp.clip(ramp_trial / dual_step, -ramp_limit, ramp_limit)
        balance_row = balance * (lax.optimization_barrier(jnp.sum(extended, axis=1)) - demand)
        price_new = balance_price + dual_step * balance_row
        if iteration < ITERS - 1:
            primal_sq = jnp.sum((moved - levels) ** 2)
            dual_sq = jnp.sum((dual_new - flow_dual) ** 2) + jnp.sum((ramp_new - ramp_dual) ** 2) + jnp.sum((price_new - balance_price) ** 2)
            weight = jnp.sqrt(weight) * ((dual_sq + 1e-06) / (primal_sq + 1e-06)) ** 0.25
        levels = moved
        flow_dual = dual_new
        ramp_dual = ramp_new
        balance_price = price_new
    return (levels, flow_dual, ramp_dual, balance_price)
```

```python
import functools
import math

import jax
import jax.numpy as jnp
from jax import lax
from jax.experimental import pallas as pl
from jax.experimental.pallas import tpu as pltpu
from jax.sharding import PartitionSpec as P

ITERS = 4
ROWS = 16


def send(src, dst, send_sem, recv_sem, target):
    return pltpu.make_async_remote_copy(
        src_ref=src,
        dst_ref=dst,
        send_sem=send_sem,
        recv_sem=recv_sem,
        device_id={"ctg": target},
        device_id_type=pl.DeviceIdType.MESH,
    )


def kernel(
    n, hour_rows, step_size, balance,
    tiles, gates, index, table, base, start_dual, starts, demand, units,
    out_levels, out_dual, out_ramp, out_price,
    masked, limit, dual_half, flow_acc,
    start_stage, frag_in, frag_out,
    cost, levels, ramp, extended, halo_ext, halo_ramp,
    pull_out, pull_in, ext_half, stats, price, omega,
    tile_sem, frag_send, frag_recv, fin_send, fin_recv,
    pull_send, pull_recv, ext_send, ext_recv, stat_send, stat_recv,
    halo_sems,
):
    f32 = jnp.float32
    bf16 = jnp.bfloat16
    members = ROWS // hour_rows
    groups = n // members
    chunks = n // groups
    unit_count = tiles.shape[2]
    width = unit_count // chunks
    ctgs, lines = tiles.shape[0], tiles.shape[1]
    hours = groups * ROWS
    pairs = chunks // 2

    me = lax.axis_index("ctg")
    my_chunk = lax.div(me, groups)
    my_group = lax.rem(me, groups)
    home_group = lax.div(me, members)
    home_row = lax.rem(me, members)
    my_pair = lax.div(my_chunk, 2)
    my_rows = pl.ds(pl.multiple_of(my_group * ROWS, ROWS), ROWS)
    my_lanes = pl.ds(pl.multiple_of(my_chunk * width, 128), width)

    def tile_copy(k):
        return pltpu.make_async_copy(
            tiles.at[k], masked.at[pl.ds(pl.multiple_of(k * lines, lines), lines)], tile_sem.at[k]
        )

    for k in range(ctgs):
        tile_copy(k).start()

    barrier = pltpu.get_barrier_semaphore()

    @pl.loop(1, n)
    def _(d):
        pl.semaphore_signal(
            barrier, inc=1, device_id={"ctg": lax.rem(me + d, n)}, device_id_type=pl.DeviceIdType.MESH
        )

    pl.semaphore_wait(barrier, n - 1)

    def frag_copy(c, target):
        return send(
            starts.at[:, :, pl.ds(pl.multiple_of(c * width, 128), width)],
            start_stage.at[home_row], frag_send.at[c], frag_recv.at[home_row], target,
        )

    for c in range(chunks):
        target = c * groups + home_group

        @pl.when(target != me)
        def _():
            frag_copy(c, target).start()

        @pl.when(target == me)
        def _():
            start_stage[home_row] = starts[:, :, c * width:(c + 1) * width]

    def stat_copy(slot, target, sender):
        return send(
            stats.at[slot, sender], stats.at[slot, sender],
            stat_send.at[slot % 2, target], stat_recv.at[slot % 2, sender], target,
        )

    def stat_start(slot):
        @pl.loop(1, n)
        def _(d):
            stat_copy(slot, lax.rem(me + d, n), me).start()

    def stat_wait(slot):
        @pl.loop(1, n)
        def _(d):
            peer = lax.rem(me + d, n)
            stat_copy(slot, peer, me).wait_send()
            stat_copy(slot, peer, peer).wait_recv()

    stats[0, me] = demand[...]
    stat_start(0)

    row_iota = lax.broadcasted_iota(jnp.int32, (128, 256), 0)
    values = table[...]
    part_a = values.astype(bf16)
    rest = values - part_a.astype(f32)
    part_b = rest.astype(bf16)
    part_c = (rest - part_b.astype(f32)).astype(bf16)
    for k in range(ctgs * lines // 256):
        which = index[:, k * 256:(k + 1) * 256]
        high = lax.shift_right_logical(which, 7)
        low = lax.bitwise_and(which, 127)
        blocks = table.shape[1] // 128
        got = jnp.zeros((128, 256), f32)
        for b in range(blocks):
            pick = jnp.where(row_iota + b * 128 == high, 1.0, 0.0).astype(bf16)
            for part in (part_a, part_b, part_c):
                got = got + jnp.dot(part[:, b * 128:(b + 1) * 128], pick, preferred_element_type=f32)
        limit[:, k * 256:(k + 1) * 256] = jnp.sum(
            jnp.where(row_iota == low, got, 0.0), axis=0, keepdims=True
        )

    out_dual[...] = start_dual[...]
    dual_half[...] = start_dual[...].astype(bf16)
    omega[...] = jnp.ones_like(omega)
    price[...] = jnp.zeros_like(price)

    @pl.loop(0, ctgs)
    def _(k):
        tile_copy(k).wait()
        for half in range(lines // 128):
            gate = jnp.broadcast_to(gates[k * (lines // 128) + half], (16, unit_count)).astype(bf16)
            for r in range(8):
                where = pl.ds(pl.multiple_of(k * lines + half * 128 + r * 16, 16), 16)
                masked[where, :] = masked[where, :] * gate

    for r in range(members):
        peer = my_group * members + r

        @pl.when(peer != me)
        def _():
            send(
                starts.at[:, :, pl.ds(0, width)], start_stage.at[r],
                frag_send.at[0], frag_recv.at[r], peer,
            ).wait_recv()

    for c in range(chunks):
        target = c * groups + home_group

        @pl.when(target != me)
        def _():
            frag_copy(c, target).wait_send()

    for r in range(members):
        rows = slice(r * hour_rows, (r + 1) * hour_rows)
        levels[rows, :] = start_stage[r, 0]
        cost[rows, :] = start_stage[r, 1]
        ramp[rows, :] = start_stage[r, 2]

    floor = units[0:1, my_lanes]
    ceiling = floor + units[1:2, my_lanes]
    ramp_limit = units[2:3, my_lanes]
    ramp_on = units[3:4, my_lanes]
    block_row = lax.broadcasted_iota(jnp.int32, (ROWS, width), 0)
    lane_here = lax.broadcasted_iota(jnp.int32, (ROWS, 128), 1)
    row_here = lax.broadcasted_iota(jnp.int32, (ROWS, 128), 0) + my_group * ROWS
    diagonal = lane_here == row_here
    hour_lanes = lax.broadcasted_iota(jnp.int32, (1, 128), 1) < hours
    stat_row = lax.broadcasted_iota(jnp.int32, (8, 128), 0)

    def pull_copy(it, c, g, target, sender):
        return send(
            pull_out.at[c, pl.ds(pl.multiple_of(g * ROWS, ROWS), ROWS)], pull_in.at[it, sender],
            pull_send.at[target], pull_recv.at[sender], target,
        )

    def ext_copy(it, target, sender):
        c, g = lax.div(sender, groups), lax.rem(sender, groups)
        spot = ext_half.at[it, c, pl.ds(pl.multiple_of(g * ROWS, ROWS), ROWS)]
        return send(spot, spot, ext_send.at[target], ext_recv.at[sender], target)

    def halo_ext_copy(it, target):
        return send(extended.at[pl.ds(0, 8)], halo_ext.at[it], halo_sems.at[0], halo_sems.at[1], target)

    def halo_ramp_copy(it, target):
        return send(ramp.at[pl.ds(ROWS - 8, 8)], halo_ramp.at[it], halo_sems.at[2], halo_sems.at[3], target)

    def absorb(slot, sigma):
        total = stats[slot, 0]
        for q in range(1, n):
            total = total + stats[slot, q]
        move = sigma * (balance * (total[0:1] - price[1:2]))
        move = jnp.where(hour_lanes, move, 0.0)
        price[0:1] = price[0:1] + move
        return total, jnp.sum(move * move, axis=1, keepdims=True)

    @pl.loop(0, ITERS)
    def _(it):
        @pl.when(my_group < groups - 1)
        def _():
            halo_ramp_copy(it, me + 1).start()

        @pl.loop(0, pairs)
        def _(j):
            pair = lax.rem(my_pair + 1 + j, pairs)
            lanes = pl.ds(pl.multiple_of(pair * (2 * width), 256), 2 * width)
            part = jnp.dot(dual_half[...], masked[:, lanes], preferred_element_type=f32).astype(bf16)
            for side in range(2):
                c = pair * 2 + side
                pull_out[c] = part[:, side * width:(side + 1) * width]
                for g in range(groups):
                    target = c * groups + g

                    @pl.when(target != me)
                    def _():
                        pull_copy(it, c, g, target, me).start()

        pull_in[it, me] = pull_out[my_chunk, my_rows, :]

        stat_wait(it)

        @pl.when(it == 0)
        def _():
            first = stats[0, 0]
            for q in range(1, n):
                first = first + stats[0, q]
            price[1:2] = first[0:1]

        @pl.when(it > 0)
        def _():
            old = omega[0:1, 0:1]
            total, price_sq = absorb(it, step_size * old)
            sums = jnp.sum(total, axis=1, keepdims=True)
            dual_sq = sums[3:4] + sums[2:3] + price_sq
            ratio = (dual_sq + 1e-06) / (sums[1:2] + 1e-06)
            omega[...] = jnp.broadcast_to(jnp.sqrt(old) * jnp.sqrt(jnp.sqrt(ratio)), omega.shape)

        weight = omega[0:1, 0:1]
        tau = step_size / weight
        sigma = step_size * weight

        @pl.loop(1, n)
        def _(d):
            peer = lax.rem(me + d, n)
            pull_copy(it, lax.div(peer, groups), lax.rem(peer, groups), peer, me).wait_send()
            pull_copy(it, 0, 0, peer, peer).wait_recv()

        pulled = pull_in[it, 0].astype(f32)
        for q in range(1, n):
            pulled = pulled + pull_in[it, q].astype(f32)

        @pl.when(my_group < groups - 1)
        def _():
            halo_ramp_copy(it, me + 1).wait_send()

        @pl.when(my_group > 0)
        def _():
            halo_ramp_copy(it, me - 1).wait_recv()

        @pl.when(my_group == 0)
        def _():
            halo_ramp[it] = jnp.zeros_like(halo_ramp[it])

        ramp_now = ramp[...]
        before = jnp.where(block_row == 0, halo_ramp[it][7:8], pltpu.roll(ramp_now, 1, 0))
        price_here = jnp.sum(
            jnp.where(diagonal, jnp.broadcast_to(price[0:1], (ROWS, 128)), 0.0), axis=1, keepdims=True
        )
        gradient = cost[...] + pulled + ramp_on * (before - ramp_now) + balance * price_here
        old_levels = levels[...]
        moved = jnp.clip(old_levels - tau * gradient, floor, ceiling)
        ext = 2.0 * moved - old_levels
        levels[...] = moved
        ext_half[it, my_chunk, my_rows, :] = ext.astype(bf16)
        extended[...] = ext

        @pl.loop(1, n)
        def _(d):
            ext_copy(it, lax.rem(me + d, n), me).start()

        @pl.when(my_group > 0)
        def _():
            halo_ext_copy(it, me - 1).start()
            halo_ext_copy(it, me - 1).wait_send()

        @pl.when(my_group < groups - 1)
        def _():
            halo_ext_copy(it, me + 1).wait_recv()

        @pl.when(my_group == groups - 1)
        def _():
            halo_ext[it] = jnp.zeros_like(halo_ext[it])

        after = jnp.where(block_row == ROWS - 1, halo_ext[it][0:1], pltpu.roll(ext, ROWS - 1, 0))
        change = ramp_on * (after - ext)
        last_hour = block_row + my_group * ROWS == hours - 1
        change = jnp.where(last_hour, 0.0, change)
        trial = ramp_now + sigma * change
        ramp_new = trial - sigma * jnp.clip(trial / sigma, -ramp_limit, ramp_limit)
        ramp[...] = ramp_new

        def lane_sums(x):
            x = jnp.sum(x, axis=0, keepdims=True)
            out = x[:, 0:128]
            for b in range(1, width // 128):
                out = out + x[:, b * 128:(b + 1) * 128]
            return out

        row_sums = jnp.sum(ext, axis=1, keepdims=True)
        row_sums = jnp.sum(
            jnp.where(diagonal, jnp.broadcast_to(row_sums, (ROWS, 128)), 0.0), axis=0, keepdims=True
        )
        primal_sq = lane_sums((moved - old_levels) ** 2)
        ramp_sq = lane_sums((ramp_new - ramp_now) ** 2)
        report = jnp.where(
            stat_row == 0, row_sums,
            jnp.where(stat_row == 1, primal_sq, jnp.where(stat_row == 2, ramp_sq, 0.0)),
        )

        @pl.when(it == ITERS - 1)
        def _():
            stats[it + 1, me] = report
            stat_start(it + 1)
            for r in range(members):
                rows = slice(r * hour_rows, (r + 1) * hour_rows)
                frag_out[r, 0] = moved[rows, :]
                frag_out[r, 1] = ramp_new[rows, :]
            for r in range(members):
                target = my_group * members + r

                @pl.when(target != me)
                def _():
                    send(
                        frag_out.at[r], frag_in.at[my_chunk], fin_send.at[r], fin_recv.at[my_chunk], target
                    ).start()

                @pl.when(target == me)
                def _():
                    frag_in[my_chunk] = frag_out[r]

        @pl.loop(0, pairs)
        def _(j):
            pair = lax.rem(my_pair + j, pairs)
            for side in range(2):
                for g in range(groups):
                    peer = (pair * 2 + side) * groups + g

                    @pl.when(peer != me)
                    def _():
                        ext_copy(it, peer, peer).wait_recv()

            lanes = pl.ds(pl.multiple_of(pair * (2 * width), 256), 2 * width)
            x = jnp.concatenate([ext_half[it, pair * 2], ext_half[it, pair * 2 + 1]], axis=1)
            part = lax.dot_general(
                x, masked[:, lanes], (((1,), (1,)), ((), ())), preferred_element_type=f32
            )

            @pl.when(j == 0)
            def _():
                flow_acc[...] = part

            @pl.when(j > 0)
            def _():
                flow_acc[...] += part

        @pl.loop(1, n)
        def _(d):
            ext_copy(it, lax.rem(me + d, n), me).wait_send()

        old_dual = out_dual[...]
        trial = old_dual + sigma * flow_acc[...]
        bound = limit[...]
        dual_new = trial - sigma * jnp.clip(trial / sigma, base[...] - bound, base[...] + bound)
        out_dual[...] = dual_new
        dual_half[...] = dual_new.astype(bf16)

        @pl.when(it < ITERS - 1)
        def _():
            moved_sq = jnp.sum((dual_new - old_dual) ** 2, axis=0, keepdims=True)
            flow_sq = moved_sq[:, 0:128]
            for b in range(1, ctgs * lines // 128):
                flow_sq = flow_sq + moved_sq[:, b * 128:(b + 1) * 128]
            stats[it + 1, me] = jnp.where(stat_row == 3, flow_sq, report)
            stat_start(it + 1)

    stat_wait(ITERS)
    absorb(ITERS, step_size * omega[0:1, 0:1])
    out_price[...] = price[...]
    for r in range(members):
        target = my_group * members + r

        @pl.when(target != me)
        def _():
            send(
                frag_out.at[r], frag_in.at[my_chunk], fin_send.at[r], fin_recv.at[my_chunk], target
            ).wait_send()

    for c in range(chunks):
        peer = c * groups + home_group

        @pl.when(peer != me)
        def _():
            send(frag_out.at[0], frag_in.at[c], fin_send.at[0], fin_recv.at[c], peer).wait_recv()

    for c in range(chunks):
        out_levels[:, c * width:(c + 1) * width] = frag_in[c, 0]
        out_ramp[:, c * width:(c + 1) * width] = frag_in[c, 1]


def body(
    flow_tiles,
    tile_pattern,
    monitored,
    ratings,
    base_flow,
    unit_cost,
    unit_floor,
    unit_span,
    ramp_limit,
    ramp_mask,
    demand,
    start_output,
    start_flow_dual,
    start_ramp_dual,
):
    f32, bf16 = jnp.float32, jnp.bfloat16
    ctgs, lines, unit_count = flow_tiles.shape
    n = lax.axis_size("ctg")
    position = lax.axis_index("ctg")
    hour_rows = start_output.shape[0]
    hours = hour_rows * n
    groups = hours // ROWS
    chunks = n // groups
    members = ROWS // hour_rows
    width = unit_count // chunks
    flat = ctgs * lines
    step_size = 0.5 / (2.0 + math.sqrt(ctgs * n * lines / unit_count))
    balance = 1.0 / math.sqrt(unit_count)

    gates = jnp.repeat(tile_pattern.astype(f32).reshape(-1, unit_count // 128), 128, axis=1)[:, None, :]
    index = monitored.reshape(1, flat)
    table = ratings.reshape(-1, 128).T
    base = base_flow.reshape(hours, flat)
    start_dual = start_flow_dual.reshape(hours, flat)
    starts = jnp.stack([start_output, unit_cost, start_ramp_dual])
    hour = lax.broadcasted_iota(jnp.int32, (8, 128), 1) - position * hour_rows
    top = lax.broadcasted_iota(jnp.int32, (8, 128), 0) == 0
    own_demand = jnp.zeros((8, 128), f32)
    for r in range(hour_rows):
        own_demand = jnp.where(top & (hour == r), demand[r], own_demand)
    units = jnp.stack([unit_floor, unit_span, ramp_limit, ramp_mask.astype(f32)])

    vmem = pl.BlockSpec(memory_space=pltpu.VMEM)
    sem = pltpu.SemaphoreType.DMA
    out = pl.pallas_call(
        functools.partial(kernel, n, hour_rows, step_size, balance),
        out_shape=(
            jax.ShapeDtypeStruct((hour_rows, unit_count), f32),
            jax.ShapeDtypeStruct((hours, flat), f32),
            jax.ShapeDtypeStruct((hour_rows, unit_count), f32),
            jax.ShapeDtypeStruct((8, 128), f32),
        ),
        in_specs=[pl.BlockSpec(memory_space=pl.ANY)] + [vmem] * 8,
        out_specs=(vmem,) * 4,
        scratch_shapes=[
            pltpu.VMEM((flat, unit_count), bf16),
            pltpu.VMEM((1, flat), f32),
            pltpu.VMEM((hours, flat), bf16),
            pltpu.VMEM((hours, flat), f32),
            pltpu.VMEM((members, 3, hour_rows, width), f32),
            pltpu.VMEM((chunks, 2, hour_rows, width), f32),
            pltpu.VMEM((members, 2, hour_rows, width), f32),
            pltpu.VMEM((ROWS, width), f32),
            pltpu.VMEM((ROWS, width), f32),
            pltpu.VMEM((ROWS, width), f32),
            pltpu.VMEM((ROWS, width), f32),
            pltpu.VMEM((ITERS, 8, width), f32),
            pltpu.VMEM((ITERS, 8, width), f32),
            pltpu.VMEM((chunks, hours, width), bf16),
            pltpu.VMEM((ITERS, n, ROWS, width), bf16),
            pltpu.VMEM((ITERS, chunks, hours, width), bf16),
            pltpu.VMEM((ITERS + 1, n, 8, 128), f32),
            pltpu.VMEM((8, 128), f32),
            pltpu.VMEM((8, 128), f32),
            sem((ctgs,)),
            sem((chunks,)), sem((members,)), sem((members,)), sem((chunks,)),
            sem((n,)), sem((n,)), sem((n,)), sem((n,)), sem((2, n)), sem((2, n)),
            sem((4,)),
        ],
        compiler_params=pltpu.CompilerParams(collective_id=0, has_side_effects=True),
    )(flow_tiles, gates, index, table, base, start_dual, starts, own_demand, units)
    own_levels, flow_dual, own_ramp, price = out
    own_price = lax.dynamic_slice_in_dim(price[0], position * hour_rows, hour_rows, 0)
    return (own_levels, flow_dual.reshape(hours, ctgs, lines), own_ramp, own_price)


def solution(mesh):
    return jax.shard_map(
        body,
        mesh=mesh,
        in_specs=(
            P("ctg", None, None),
            P("ctg", None, None),
            P("ctg", None),
            P(),
            P("grp", "ctg", None),
            P(("grp", "ctg"), None),
            P(),
            P(),
            P(),
            P(),
            P(("grp", "ctg")),
            P(("grp", "ctg"), None),
            P("grp", "ctg", None),
            P(("grp", "ctg"), None),
        ),
        out_specs=(
            P(("grp", "ctg"), None),
            P("grp", "ctg", None),
            P(("grp", "ctg"), None),
            P(("grp", "ctg")),
        ),
        check_vma=False,
    )
```

```python
import functools
import math

import jax
import jax.numpy as jnp
from jax import lax
from jax.experimental import pallas as pl
from jax.experimental.pallas import tpu as pltpu
from jax.sharding import PartitionSpec as P

ITERS = 4
ROWS = 16


def send(src, dst, send_sem, recv_sem, target):
    return pltpu.make_async_remote_copy(
        src_ref=src,
        dst_ref=dst,
        send_sem=send_sem,
        recv_sem=recv_sem,
        device_id={"ctg": target},
        device_id_type=pl.DeviceIdType.MESH,
    )


def kernel(
    n, hour_rows, step_size, balance,
    tiles, pattern, index, table, base_in, dual_in, level_in, cost_in, ramp_in, demand,
    floor_in, span_in, ramp_limit_in, ramp_mask_in,
    out_levels, out_dual, out_ramp, out_price,
    masked, base, starts, limit, dual_half, flow_acc,
    start_stage, frag_in, frag_out,
    cost, levels, ramp, extended, halo_ext, halo_ramp,
    pull_out, pull_in, ext_half, stats, price, omega,
    tile_sem, frag_send, frag_recv, fin_send, fin_recv,
    pull_send, pull_recv, ext_send, ext_recv, stat_send, stat_recv,
    halo_sems,
):
    f32 = jnp.float32
    bf16 = jnp.bfloat16
    members = ROWS // hour_rows
    groups = n // members
    chunks = n // groups
    unit_count = tiles.shape[2]
    width = unit_count // chunks
    ctgs, lines = tiles.shape[0], tiles.shape[1]
    hours = groups * ROWS
    pairs = chunks // 2

    me = lax.axis_index("ctg")
    my_chunk = lax.div(me, groups)
    my_group = lax.rem(me, groups)
    home_group = lax.div(me, members)
    home_row = lax.rem(me, members)
    my_pair = lax.div(my_chunk, 2)
    my_rows = pl.ds(pl.multiple_of(my_group * ROWS, ROWS), ROWS)
    my_lanes = pl.ds(pl.multiple_of(my_chunk * width, 128), width)

    def tile_copy(k):
        return pltpu.make_async_copy(
            tiles.at[k], masked.at[pl.ds(pl.multiple_of(k * lines, lines), lines)], tile_sem.at[k]
        )

    for k in range(ctgs):
        tile_copy(k).start()

    barrier = pltpu.get_barrier_semaphore()

    @pl.loop(1, n)
    def _(d):
        pl.semaphore_signal(
            barrier, inc=1, device_id={"ctg": lax.rem(me + d, n)}, device_id_type=pl.DeviceIdType.MESH
        )

    pl.semaphore_wait(barrier, n - 1)

    def frag_copy(c, target):
        return send(
            starts.at[:, :, pl.ds(pl.multiple_of(c * width, 128), width)],
            start_stage.at[home_row], frag_send.at[c], frag_recv.at[home_row], target,
        )

    starts[0] = level_in[...]
    starts[1] = cost_in[...]
    starts[2] = ramp_in[...]
    for c in range(chunks):
        target = c * groups + home_group

        @pl.when(target != me)
        def _():
            frag_copy(c, target).start()

        @pl.when(target == me)
        def _():
            start_stage[home_row] = starts[:, :, c * width:(c + 1) * width]

    def stat_copy(slot, target, sender):
        return send(
            stats.at[slot, sender], stats.at[slot, sender],
            stat_send.at[slot % 2, target], stat_recv.at[slot % 2, sender], target,
        )

    def stat_start(slot):
        @pl.loop(1, n)
        def _(d):
            stat_copy(slot, lax.rem(me + d, n), me).start()

    def stat_wait(slot):
        @pl.loop(1, n)
        def _(d):
            peer = lax.rem(me + d, n)
            stat_copy(slot, peer, me).wait_send()
            stat_copy(slot, peer, peer).wait_recv()

    hour = lax.broadcasted_iota(jnp.int32, (8, 128), 1) - me * hour_rows
    own_demand = jnp.zeros((8, 128), f32)
    for r in range(hour_rows):
        own_demand = jnp.where(hour == r, demand[r], own_demand)
    stats[0, me] = own_demand
    stat_start(0)

    row_iota = lax.broadcasted_iota(jnp.int32, (128, lines), 0)
    values = table[...].T
    part_a = values.astype(bf16)
    rest = values - part_a.astype(f32)
    part_b = rest.astype(bf16)
    part_c = (rest - part_b.astype(f32)).astype(bf16)
    for k in range(ctgs):
        which = index[k:k + 1, :]
        high = lax.shift_right_logical(which, 7)
        low = lax.bitwise_and(which, 127)
        blocks = table.shape[0] // 128
        got = jnp.zeros((128, lines), f32)
        for b in range(blocks):
            pick = jnp.where(row_iota + b * 128 == high, 1.0, 0.0).astype(bf16)
            for part in (part_a, part_b, part_c):
                got = got + jnp.dot(part[:, b * 128:(b + 1) * 128], pick, preferred_element_type=f32)
        limit[:, k * lines:(k + 1) * lines] = jnp.sum(
            jnp.where(row_iota == low, got, 0.0), axis=0, keepdims=True
        )

    for k in range(ctgs):
        lanes = slice(k * lines, (k + 1) * lines)
        base[:, lanes] = base_in[:, k, :]
        dual = dual_in[:, k, :]
        out_dual[:, lanes] = dual
        dual_half[:, lanes] = dual.astype(bf16)
    omega[...] = jnp.ones_like(omega)
    price[...] = jnp.zeros_like(price)

    tile_count = unit_count // 128
    tile_row = lax.broadcasted_iota(jnp.int32, (tile_count, unit_count), 0)
    tile_lane = lax.broadcasted_iota(jnp.int32, (tile_count, unit_count), 1)
    spread = jnp.where(lax.shift_right_logical(tile_lane, 7) == tile_row, 1.0, 0.0)

    @pl.loop(0, ctgs)
    def _(k):
        tile_copy(k).wait()
        gates = jnp.dot(pattern[k].astype(f32), spread, preferred_element_type=f32)
        for half in range(lines // 128):
            gate = jnp.broadcast_to(gates[half:half + 1], (16, unit_count)).astype(bf16)
            for r in range(8):
                where = pl.ds(pl.multiple_of(k * lines + half * 128 + r * 16, 16), 16)
                masked[where, :] = masked[where, :] * gate

    for r in range(members):
        peer = my_group * members + r

        @pl.when(peer != me)
        def _():
            send(
                starts.at[:, :, pl.ds(0, width)], start_stage.at[r],
                frag_send.at[0], frag_recv.at[r], peer,
            ).wait_recv()

    for c in range(chunks):
        target = c * groups + home_group

        @pl.when(target != me)
        def _():
            frag_copy(c, target).wait_send()

    for r in range(members):
        rows = slice(r * hour_rows, (r + 1) * hour_rows)
        levels[rows, :] = start_stage[r, 0]
        cost[rows, :] = start_stage[r, 1]
        ramp[rows, :] = start_stage[r, 2]

    floor = floor_in[:, my_lanes]
    ceiling = floor + span_in[:, my_lanes]
    ramp_limit = ramp_limit_in[:, my_lanes]
    ramp_on = ramp_mask_in[:, my_lanes].astype(f32)
    block_row = lax.broadcasted_iota(jnp.int32, (ROWS, width), 0)
    lane_here = lax.broadcasted_iota(jnp.int32, (ROWS, 128), 1)
    row_here = lax.broadcasted_iota(jnp.int32, (ROWS, 128), 0) + my_group * ROWS
    diagonal = lane_here == row_here
    hour_lanes = lax.broadcasted_iota(jnp.int32, (1, 128), 1) < hours
    stat_row = lax.broadcasted_iota(jnp.int32, (8, 128), 0)

    def pull_copy(it, c, g, target, sender):
        return send(
            pull_out.at[c, pl.ds(pl.multiple_of(g * ROWS, ROWS), ROWS)], pull_in.at[it, sender],
            pull_send.at[target], pull_recv.at[sender], target,
        )

    def ext_copy(it, target, sender):
        c, g = lax.div(sender, groups), lax.rem(sender, groups)
        spot = ext_half.at[it, c, pl.ds(pl.multiple_of(g * ROWS, ROWS), ROWS)]
        return send(spot, spot, ext_send.at[target], ext_recv.at[sender], target)

    def halo_ext_copy(it, target):
        return send(extended.at[pl.ds(0, 8)], halo_ext.at[it], halo_sems.at[0], halo_sems.at[1], target)

    def halo_ramp_copy(it, target):
        return send(ramp.at[pl.ds(ROWS - 8, 8)], halo_ramp.at[it], halo_sems.at[2], halo_sems.at[3], target)

    def absorb(slot, sigma):
        total = stats[slot, 0]
        for q in range(1, n):
            total = total + stats[slot, q]
        move = sigma * (balance * (total[0:1] - price[1:2]))
        move = jnp.where(hour_lanes, move, 0.0)
        price[0:1] = price[0:1] + move
        return total, jnp.sum(move * move, axis=1, keepdims=True)

    @pl.loop(0, ITERS)
    def _(it):
        @pl.when(my_group < groups - 1)
        def _():
            halo_ramp_copy(it, me + 1).start()

        @pl.loop(0, pairs)
        def _(j):
            pair = lax.rem(my_pair + 1 + j, pairs)
            lanes = pl.ds(pl.multiple_of(pair * (2 * width), 256), 2 * width)
            part = jnp.dot(dual_half[...], masked[:, lanes], preferred_element_type=f32).astype(bf16)
            for side in range(2):
                c = pair * 2 + side
                pull_out[c] = part[:, side * width:(side + 1) * width]
                for g in range(groups):
                    target = c * groups + g

                    @pl.when(target != me)
                    def _():
                        pull_copy(it, c, g, target, me).start()

        pull_in[it, me] = pull_out[my_chunk, my_rows, :]

        stat_wait(it)

        @pl.when(it == 0)
        def _():
            first = stats[0, 0]
            for q in range(1, n):
                first = first + stats[0, q]
            price[1:2] = first[0:1]

        @pl.when(it > 0)
        def _():
            old = omega[0:1, 0:1]
            total, price_sq = absorb(it, step_size * old)
            sums = jnp.sum(total, axis=1, keepdims=True)
            dual_sq = sums[3:4] + sums[2:3] + price_sq
            ratio = (dual_sq + 1e-06) / (sums[1:2] + 1e-06)
            omega[...] = jnp.broadcast_to(jnp.sqrt(old) * jnp.sqrt(jnp.sqrt(ratio)), omega.shape)

        weight = omega[0:1, 0:1]
        tau = step_size / weight
        sigma = step_size * weight

        @pl.loop(1, n)
        def _(d):
            peer = lax.rem(me + d, n)
            pull_copy(it, lax.div(peer, groups), lax.rem(peer, groups), peer, me).wait_send()
            pull_copy(it, 0, 0, peer, peer).wait_recv()

        pulled = pull_in[it, 0].astype(f32)
        for q in range(1, n):
            pulled = pulled + pull_in[it, q].astype(f32)

        @pl.when(my_group < groups - 1)
        def _():
            halo_ramp_copy(it, me + 1).wait_send()

        @pl.when(my_group > 0)
        def _():
            halo_ramp_copy(it, me - 1).wait_recv()

        @pl.when(my_group == 0)
        def _():
            halo_ramp[it] = jnp.zeros_like(halo_ramp[it])

        ramp_now = ramp[...]
        before = jnp.where(block_row == 0, halo_ramp[it][7:8], pltpu.roll(ramp_now, 1, 0))
        price_here = jnp.sum(
            jnp.where(diagonal, jnp.broadcast_to(price[0:1], (ROWS, 128)), 0.0), axis=1, keepdims=True
        )
        gradient = cost[...] + pulled + ramp_on * (before - ramp_now) + balance * price_here
        old_levels = levels[...]
        moved = jnp.clip(old_levels - tau * gradient, floor, ceiling)
        ext = 2.0 * moved - old_levels
        levels[...] = moved
        ext_half[it, my_chunk, my_rows, :] = ext.astype(bf16)
        extended[...] = ext

        @pl.loop(1, n)
        def _(d):
            ext_copy(it, lax.rem(me + d, n), me).start()

        @pl.when(my_group > 0)
        def _():
            halo_ext_copy(it, me - 1).start()
            halo_ext_copy(it, me - 1).wait_send()

        @pl.when(my_group < groups - 1)
        def _():
            halo_ext_copy(it, me + 1).wait_recv()

        @pl.when(my_group == groups - 1)
        def _():
            halo_ext[it] = jnp.zeros_like(halo_ext[it])

        after = jnp.where(block_row == ROWS - 1, halo_ext[it][0:1], pltpu.roll(ext, ROWS - 1, 0))
        change = ramp_on * (after - ext)
        last_hour = block_row + my_group * ROWS == hours - 1
        change = jnp.where(last_hour, 0.0, change)
        trial = ramp_now + sigma * change
        ramp_new = trial - sigma * jnp.clip(trial / sigma, -ramp_limit, ramp_limit)
        ramp[...] = ramp_new

        def lane_sums(x):
            x = jnp.sum(x, axis=0, keepdims=True)
            out = x[:, 0:128]
            for b in range(1, width // 128):
                out = out + x[:, b * 128:(b + 1) * 128]
            return out

        row_sums = jnp.sum(ext, axis=1, keepdims=True)
        row_sums = jnp.sum(
            jnp.where(diagonal, jnp.broadcast_to(row_sums, (ROWS, 128)), 0.0), axis=0, keepdims=True
        )
        primal_sq = lane_sums((moved - old_levels) ** 2)
        ramp_sq = lane_sums((ramp_new - ramp_now) ** 2)
        report = jnp.where(
            stat_row == 0, row_sums,
            jnp.where(stat_row == 1, primal_sq, jnp.where(stat_row == 2, ramp_sq, 0.0)),
        )

        @pl.when(it == ITERS - 1)
        def _():
            stats[it + 1, me] = report
            stat_start(it + 1)
            for r in range(members):
                rows = slice(r * hour_rows, (r + 1) * hour_rows)
                frag_out[r, 0] = moved[rows, :]
                frag_out[r, 1] = ramp_new[rows, :]
            for r in range(members):
                target = my_group * members + r

                @pl.when(target != me)
                def _():
                    send(
                        frag_out.at[r], frag_in.at[my_chunk], fin_send.at[r], fin_recv.at[my_chunk], target
                    ).start()

                @pl.when(target == me)
                def _():
                    frag_in[my_chunk] = frag_out[r]

        @pl.loop(0, pairs)
        def _(j):
            pair = lax.rem(my_pair + j, pairs)
            for side in range(2):
                for g in range(groups):
                    peer = (pair * 2 + side) * groups + g

                    @pl.when(peer != me)
                    def _():
                        ext_copy(it, peer, peer).wait_recv()

            lanes = pl.ds(pl.multiple_of(pair * (2 * width), 256), 2 * width)
            x = jnp.concatenate([ext_half[it, pair * 2], ext_half[it, pair * 2 + 1]], axis=1)
            part = lax.dot_general(
                x, masked[:, lanes], (((1,), (1,)), ((), ())), preferred_element_type=f32
            )

            @pl.when(j == 0)
            def _():
                flow_acc[...] = part

            @pl.when(j > 0)
            def _():
                flow_acc[...] += part

        @pl.loop(1, n)
        def _(d):
            ext_copy(it, lax.rem(me + d, n), me).wait_send()

        old_dual = out_dual[...]
        trial = old_dual + sigma * flow_acc[...]
        bound = limit[...]
        dual_new = trial - sigma * jnp.clip(trial / sigma, base[...] - bound, base[...] + bound)
        out_dual[...] = dual_new
        dual_half[...] = dual_new.astype(bf16)

        @pl.when(it < ITERS - 1)
        def _():
            moved_sq = jnp.sum((dual_new - old_dual) ** 2, axis=0, keepdims=True)
            flow_sq = moved_sq[:, 0:128]
            for b in range(1, ctgs * lines // 128):
                flow_sq = flow_sq + moved_sq[:, b * 128:(b + 1) * 128]
            stats[it + 1, me] = jnp.where(stat_row == 3, flow_sq, report)
            stat_start(it + 1)

    stat_wait(ITERS)
    absorb(ITERS, step_size * omega[0:1, 0:1])
    out_price[...] = price[...]
    for r in range(members):
        target = my_group * members + r

        @pl.when(target != me)
        def _():
            send(
                frag_out.at[r], frag_in.at[my_chunk], fin_send.at[r], fin_recv.at[my_chunk], target
            ).wait_send()

    for c in range(chunks):
        peer = c * groups + home_group

        @pl.when(peer != me)
        def _():
            send(frag_out.at[0], frag_in.at[c], fin_send.at[0], fin_recv.at[c], peer).wait_recv()

    for c in range(chunks):
        out_levels[:, c * width:(c + 1) * width] = frag_in[c, 0]
        out_ramp[:, c * width:(c + 1) * width] = frag_in[c, 1]


def finish(levels, dual, ramp, price, out_levels, out_dual, out_ramp, out_price):
    lines = out_dual.shape[2]
    out_levels[...] = levels[...]
    out_ramp[...] = ramp[...]
    for k in range(out_dual.shape[1]):
        out_dual[:, k, :] = dual[:, k * lines:(k + 1) * lines]
    hour_rows = out_price.shape[0]
    lane = lax.broadcasted_iota(jnp.int32, (1, 128), 1) - lax.axis_index("ctg") * hour_rows
    for r in range(hour_rows):
        out_price[r] = jnp.sum(jnp.where(lane == r, price[0:1], 0.0))


def body(
    flow_tiles,
    tile_pattern,
    monitored,
    ratings,
    base_flow,
    unit_cost,
    unit_floor,
    unit_span,
    ramp_limit,
    ramp_mask,
    demand,
    start_output,
    start_flow_dual,
    start_ramp_dual,
):
    f32, bf16 = jnp.float32, jnp.bfloat16
    ctgs, lines, unit_count = flow_tiles.shape
    n = lax.axis_size("ctg")
    hour_rows = start_output.shape[0]
    hours = hour_rows * n
    groups = hours // ROWS
    chunks = n // groups
    members = ROWS // hour_rows
    width = unit_count // chunks
    flat = ctgs * lines
    step_size = 0.5 / (2.0 + math.sqrt(ctgs * n * lines / unit_count))
    balance = 1.0 / math.sqrt(unit_count)

    vmem = pl.BlockSpec(memory_space=pltpu.VMEM)
    sem = pltpu.SemaphoreType.DMA
    out = pl.pallas_call(
        functools.partial(kernel, n, hour_rows, step_size, balance),
        out_shape=(
            jax.ShapeDtypeStruct((hour_rows, unit_count), f32),
            jax.ShapeDtypeStruct((hours, flat), f32),
            jax.ShapeDtypeStruct((hour_rows, unit_count), f32),
            jax.ShapeDtypeStruct((8, 128), f32),
        ),
        in_specs=[pl.BlockSpec(memory_space=pl.ANY)]
        + [vmem] * 8
        + [pl.BlockSpec(memory_space=pltpu.SMEM)]
        + [vmem] * 4,
        out_specs=(vmem,) * 4,
        scratch_shapes=[
            pltpu.VMEM((flat, unit_count), bf16),
            pltpu.VMEM((hours, flat), f32),
            pltpu.VMEM((3, hour_rows, unit_count), f32),
            pltpu.VMEM((1, flat), f32),
            pltpu.VMEM((hours, flat), bf16),
            pltpu.VMEM((hours, flat), f32),
            pltpu.VMEM((members, 3, hour_rows, width), f32),
            pltpu.VMEM((chunks, 2, hour_rows, width), f32),
            pltpu.VMEM((members, 2, hour_rows, width), f32),
            pltpu.VMEM((ROWS, width), f32),
            pltpu.VMEM((ROWS, width), f32),
            pltpu.VMEM((ROWS, width), f32),
            pltpu.VMEM((ROWS, width), f32),
            pltpu.VMEM((ITERS, 8, width), f32),
            pltpu.VMEM((ITERS, 8, width), f32),
            pltpu.VMEM((chunks, hours, width), bf16),
            pltpu.VMEM((ITERS, n, ROWS, width), bf16),
            pltpu.VMEM((ITERS, chunks, hours, width), bf16),
            pltpu.VMEM((ITERS + 1, n, 8, 128), f32),
            pltpu.VMEM((8, 128), f32),
            pltpu.VMEM((8, 128), f32),
            sem((ctgs,)),
            sem((chunks,)), sem((members,)), sem((members,)), sem((chunks,)),
            sem((n,)), sem((n,)), sem((n,)), sem((n,)), sem((2, n)), sem((2, n)),
            sem((4,)),
        ],
        compiler_params=pltpu.CompilerParams(collective_id=0, has_side_effects=True),
    )(
        flow_tiles,
        tile_pattern,
        monitored,
        ratings.reshape(-1, 128),
        base_flow,
        start_flow_dual,
        start_output,
        unit_cost,
        start_ramp_dual,
        demand,
        unit_floor[None],
        unit_span[None],
        ramp_limit[None],
        ramp_mask[None],
    )
    return pl.pallas_call(
        finish,
        out_shape=(
            jax.ShapeDtypeStruct((hour_rows, unit_count), f32),
            jax.ShapeDtypeStruct((hours, ctgs, lines), f32),
            jax.ShapeDtypeStruct((hour_rows, unit_count), f32),
            jax.ShapeDtypeStruct((hour_rows,), f32),
        ),
        in_specs=[vmem] * 4,
        out_specs=(vmem,) * 3 + (pl.BlockSpec(memory_space=pltpu.SMEM),),
    )(*out)


def solution(mesh):
    return jax.shard_map(
        body,
        mesh=mesh,
        in_specs=(
            P("ctg", None, None),
            P("ctg", None, None),
            P("ctg", None),
            P(),
            P("grp", "ctg", None),
            P(("grp", "ctg"), None),
            P(),
            P(),
            P(),
            P(),
            P(("grp", "ctg")),
            P(("grp", "ctg"), None),
            P("grp", "ctg", None),
            P(("grp", "ctg"), None),
        ),
        out_specs=(
            P(("grp", "ctg"), None),
            P("grp", "ctg", None),
            P(("grp", "ctg"), None),
            P(("grp", "ctg")),
        ),
        check_vma=False,
    )
```

```python
import functools
import math

import jax
import jax.numpy as jnp
from jax import lax
from jax.experimental import pallas as pl
from jax.experimental.pallas import tpu as pltpu
from jax.sharding import PartitionSpec as P

ITERS = 4
ROWS = 16


def send(src, dst, send_sem, recv_sem, target):
    return pltpu.make_async_remote_copy(
        src_ref=src,
        dst_ref=dst,
        send_sem=send_sem,
        recv_sem=recv_sem,
        device_id={"ctg": target},
        device_id_type=pl.DeviceIdType.MESH,
    )


def kernel(
    n, hour_rows, step_size, balance,
    tiles, pattern, index, table, base_in, dual_in, level_in, cost_in, ramp_in, demand,
    floor_in, span_in, ramp_limit_in, ramp_mask_in,
    out_levels, out_dual, out_ramp, out_price,
    masked, base, starts, limit, dual_half, flow_acc,
    start_stage, frag_in, frag_out,
    cost, levels, ramp, extended, halo_ext, halo_ramp,
    pull_out, pair_in, pull_sum, pull_in, ext_half, stats, price, omega,
    tile_sem, frag_send, frag_recv, fin_send, fin_recv,
    pair_send, pair_recv, pull_send, pull_recv, ext_send, ext_recv, pass_send, stat_send, stat_recv,
    halo_sems,
):
    f32 = jnp.float32
    bf16 = jnp.bfloat16
    members = ROWS // hour_rows
    groups = n // members
    chunks = n // groups
    unit_count = tiles.shape[2]
    width = unit_count // chunks
    ctgs, lines = tiles.shape[0], tiles.shape[1]
    hours = groups * ROWS
    pairs = chunks // 2

    me = lax.axis_index("ctg")
    my_chunk = lax.div(me, groups)
    my_group = lax.rem(me, groups)
    home_group = lax.div(me, members)
    home_row = lax.rem(me, members)
    my_pair = lax.div(my_chunk, 2)
    core = lax.rem(me, 2)
    chip = lax.div(me, 2)
    partner = me + 1 - 2 * core
    chips = n // 2
    my_rows = pl.ds(pl.multiple_of(my_group * ROWS, ROWS), ROWS)
    my_lanes = pl.ds(pl.multiple_of(my_chunk * width, 128), width)

    def tile_copy(k):
        return pltpu.make_async_copy(
            tiles.at[k], masked.at[pl.ds(pl.multiple_of(k * lines, lines), lines)], tile_sem.at[k]
        )

    for k in range(ctgs):
        tile_copy(k).start()

    barrier = pltpu.get_barrier_semaphore()

    @pl.loop(1, n)
    def _(d):
        pl.semaphore_signal(
            barrier, inc=1, device_id={"ctg": lax.rem(me + d, n)}, device_id_type=pl.DeviceIdType.MESH
        )

    pl.semaphore_wait(barrier, n - 1)

    def frag_copy(c, target):
        return send(
            starts.at[:, :, pl.ds(pl.multiple_of(c * width, 128), width)],
            start_stage.at[home_row], frag_send.at[c], frag_recv.at[home_row], target,
        )

    starts[0] = level_in[...]
    starts[1] = cost_in[...]
    starts[2] = ramp_in[...]
    for c in range(chunks):
        target = c * groups + home_group

        @pl.when(target != me)
        def _():
            frag_copy(c, target).start()

        @pl.when(target == me)
        def _():
            start_stage[home_row] = starts[:, :, c * width:(c + 1) * width]

    def stat_copy(slot, target, sender):
        return send(
            stats.at[slot, sender], stats.at[slot, sender],
            stat_send.at[slot % 2, target], stat_recv.at[slot % 2, sender], target,
        )

    def stat_start(slot):
        @pl.loop(1, n)
        def _(d):
            stat_copy(slot, lax.rem(me + d, n), me).start()

    def stat_wait(slot):
        @pl.loop(1, n)
        def _(d):
            peer = lax.rem(me + d, n)
            stat_copy(slot, peer, me).wait_send()
            stat_copy(slot, peer, peer).wait_recv()

    hour = lax.broadcasted_iota(jnp.int32, (8, 128), 1) - me * hour_rows
    own_demand = jnp.zeros((8, 128), f32)
    for r in range(hour_rows):
        own_demand = jnp.where(hour == r, demand[r], own_demand)
    stats[0, me] = own_demand
    stat_start(0)

    row_iota = lax.broadcasted_iota(jnp.int32, (128, lines), 0)
    values = table[...].T
    part_a = values.astype(bf16)
    rest = values - part_a.astype(f32)
    part_b = rest.astype(bf16)
    part_c = (rest - part_b.astype(f32)).astype(bf16)
    for k in range(ctgs):
        which = index[k:k + 1, :]
        high = lax.shift_right_logical(which, 7)
        low = lax.bitwise_and(which, 127)
        blocks = table.shape[0] // 128
        got = jnp.zeros((128, lines), f32)
        for b in range(blocks):
            pick = jnp.where(row_iota + b * 128 == high, 1.0, 0.0).astype(bf16)
            for part in (part_a, part_b, part_c):
                got = got + jnp.dot(part[:, b * 128:(b + 1) * 128], pick, preferred_element_type=f32)
        limit[:, k * lines:(k + 1) * lines] = jnp.sum(
            jnp.where(row_iota == low, got, 0.0), axis=0, keepdims=True
        )

    for k in range(ctgs):
        lanes = slice(k * lines, (k + 1) * lines)
        base[:, lanes] = base_in[:, k, :]
        dual = dual_in[:, k, :]
        out_dual[:, lanes] = dual
        dual_half[:, lanes] = dual.astype(bf16)
    omega[...] = jnp.ones_like(omega)
    price[...] = jnp.zeros_like(price)

    tile_count = unit_count // 128
    tile_row = lax.broadcasted_iota(jnp.int32, (tile_count, unit_count), 0)
    tile_lane = lax.broadcasted_iota(jnp.int32, (tile_count, unit_count), 1)
    spread = jnp.where(lax.shift_right_logical(tile_lane, 7) == tile_row, 1.0, 0.0)

    @pl.loop(0, ctgs)
    def _(k):
        tile_copy(k).wait()
        gates = jnp.dot(pattern[k].astype(f32), spread, preferred_element_type=f32)
        for half in range(lines // 128):
            gate = jnp.broadcast_to(gates[half:half + 1], (16, unit_count)).astype(bf16)
            for r in range(8):
                where = pl.ds(pl.multiple_of(k * lines + half * 128 + r * 16, 16), 16)
                masked[where, :] = masked[where, :] * gate

    for r in range(members):
        peer = my_group * members + r

        @pl.when(peer != me)
        def _():
            send(
                starts.at[:, :, pl.ds(0, width)], start_stage.at[r],
                frag_send.at[0], frag_recv.at[r], peer,
            ).wait_recv()

    for c in range(chunks):
        target = c * groups + home_group

        @pl.when(target != me)
        def _():
            frag_copy(c, target).wait_send()

    for r in range(members):
        rows = slice(r * hour_rows, (r + 1) * hour_rows)
        levels[rows, :] = start_stage[r, 0]
        cost[rows, :] = start_stage[r, 1]
        ramp[rows, :] = start_stage[r, 2]

    floor = floor_in[:, my_lanes]
    ceiling = floor + span_in[:, my_lanes]
    ramp_limit = ramp_limit_in[:, my_lanes]
    ramp_on = ramp_mask_in[:, my_lanes].astype(f32)
    block_row = lax.broadcasted_iota(jnp.int32, (ROWS, width), 0)
    lane_here = lax.broadcasted_iota(jnp.int32, (ROWS, 128), 1)
    row_here = lax.broadcasted_iota(jnp.int32, (ROWS, 128), 0) + my_group * ROWS
    diagonal = lane_here == row_here
    hour_lanes = lax.broadcasted_iota(jnp.int32, (1, 128), 1) < hours
    stat_row = lax.broadcasted_iota(jnp.int32, (8, 128), 0)

    def block_rows(g):
        return pl.ds(pl.multiple_of(g * ROWS, ROWS), ROWS)

    def pair_copy(it, owner):
        c, g = lax.div(owner, groups), lax.rem(owner, groups)
        return send(
            pull_out.at[c, block_rows(g)], pair_in.at[it, c, block_rows(g)],
            pair_send.at[owner], pair_recv.at[owner], partner,
        )

    def pull_copy(it, target, sender_chip):
        c, g = lax.div(target, groups), lax.rem(target, groups)
        return send(
            pull_sum.at[c, block_rows(g)], pull_in.at[it, sender_chip],
            pull_send.at[target], pull_recv.at[sender_chip], target,
        )

    def ext_copy(it, target, origin, send_sem):
        c, g = lax.div(origin, groups), lax.rem(origin, groups)
        spot = ext_half.at[it, c, block_rows(g)]
        return send(spot, spot, send_sem, ext_recv.at[origin], target)

    def ext_out(it, target):
        return ext_copy(it, target, me, ext_send.at[target])

    def ext_forward(it, origin):
        return ext_copy(it, partner, origin, pass_send.at[origin])

    def halo_ext_copy(it, target):
        return send(extended.at[pl.ds(0, 8)], halo_ext.at[it], halo_sems.at[0], halo_sems.at[1], target)

    def halo_ramp_copy(it, target):
        return send(ramp.at[pl.ds(ROWS - 8, 8)], halo_ramp.at[it], halo_sems.at[2], halo_sems.at[3], target)

    def absorb(slot, sigma):
        total = stats[slot, 0]
        for q in range(1, n):
            total = total + stats[slot, q]
        move = sigma * (balance * (total[0:1] - price[1:2]))
        move = jnp.where(hour_lanes, move, 0.0)
        price[0:1] = price[0:1] + move
        return total, jnp.sum(move * move, axis=1, keepdims=True)

    @pl.loop(0, ITERS)
    def _(it):
        @pl.when(my_group < groups - 1)
        def _():
            halo_ramp_copy(it, me + 1).start()

        @pl.loop(0, pairs + 1)
        def _(j):
            @pl.when(j < pairs)
            def _():
                pair = lax.rem(my_pair + 1 + j, pairs)
                lanes = pl.ds(pl.multiple_of(pair * (2 * width), 256), 2 * width)
                part = jnp.dot(dual_half[...], masked[:, lanes], preferred_element_type=f32).astype(bf16)
                for side in range(2):
                    c = pair * 2 + side
                    pull_out[c] = part[:, side * width:(side + 1) * width]
                    for h in range(groups // 2):
                        pair_copy(it, c * groups + 2 * h + 1 - core).start()

            @pl.when(j > 0)
            def _():
                pair = lax.rem(my_pair + j, pairs)
                for side in range(2):
                    c = pair * 2 + side
                    for h in range(groups // 2):
                        g = 2 * h + core
                        target = c * groups + g
                        pair_copy(it, target).wait_recv()
                        both = (
                            pull_out[c, block_rows(g), :].astype(f32)
                            + pair_in[it, c, block_rows(g), :].astype(f32)
                        ).astype(bf16)

                        @pl.when(target != me)
                        def _():
                            pull_sum[c, block_rows(g), :] = both
                            pull_copy(it, target, chip).start()

                        @pl.when(target == me)
                        def _():
                            pull_in[it, chip] = both

        stat_wait(it)

        @pl.when(it == 0)
        def _():
            first = stats[0, 0]
            for q in range(1, n):
                first = first + stats[0, q]
            price[1:2] = first[0:1]

        @pl.when(it > 0)
        def _():
            old = omega[0:1, 0:1]
            total, price_sq = absorb(it, step_size * old)
            sums = jnp.sum(total, axis=1, keepdims=True)
            dual_sq = sums[3:4] + sums[2:3] + price_sq
            ratio = (dual_sq + 1e-06) / (sums[1:2] + 1e-06)
            omega[...] = jnp.broadcast_to(jnp.sqrt(old) * jnp.sqrt(jnp.sqrt(ratio)), omega.shape)

        weight = omega[0:1, 0:1]
        tau = step_size / weight
        sigma = step_size * weight

        @pl.loop(1, chips)
        def _(d):
            other = lax.rem(chip + d, chips)
            pull_copy(it, other * 2 + core, chip).wait_send()
            pull_copy(it, other * 2 + core, other).wait_recv()

        @pl.loop(0, chips)
        def _(q):
            pair_copy(it, q * 2 + 1 - core).wait_send()

        pulled = pull_in[it, 0].astype(f32)
        for q in range(1, chips):
            pulled = pulled + pull_in[it, q].astype(f32)

        @pl.when(my_group < groups - 1)
        def _():
            halo_ramp_copy(it, me + 1).wait_send()

        @pl.when(my_group > 0)
        def _():
            halo_ramp_copy(it, me - 1).wait_recv()

        @pl.when(my_group == 0)
        def _():
            halo_ramp[it] = jnp.zeros_like(halo_ramp[it])

        ramp_now = ramp[...]
        before = jnp.where(block_row == 0, halo_ramp[it][7:8], pltpu.roll(ramp_now, 1, 0))
        price_here = jnp.sum(
            jnp.where(diagonal, jnp.broadcast_to(price[0:1], (ROWS, 128)), 0.0), axis=1, keepdims=True
        )
        gradient = cost[...] + pulled + ramp_on * (before - ramp_now) + balance * price_here
        old_levels = levels[...]
        moved = jnp.clip(old_levels - tau * gradient, floor, ceiling)
        ext = 2.0 * moved - old_levels
        levels[...] = moved
        ext_half[it, my_chunk, my_rows, :] = ext.astype(bf16)
        extended[...] = ext

        @pl.loop(1, chips)
        def _(d):
            ext_out(it, lax.rem(chip + d, chips) * 2 + core).start()

        ext_out(it, partner).start()

        @pl.when(my_group > 0)
        def _():
            halo_ext_copy(it, me - 1).start()
            halo_ext_copy(it, me - 1).wait_send()

        @pl.when(my_group < groups - 1)
        def _():
            halo_ext_copy(it, me + 1).wait_recv()

        @pl.when(my_group == groups - 1)
        def _():
            halo_ext[it] = jnp.zeros_like(halo_ext[it])

        after = jnp.where(block_row == ROWS - 1, halo_ext[it][0:1], pltpu.roll(ext, ROWS - 1, 0))
        change = ramp_on * (after - ext)
        last_hour = block_row + my_group * ROWS == hours - 1
        change = jnp.where(last_hour, 0.0, change)
        trial = ramp_now + sigma * change
        ramp_new = trial - sigma * jnp.clip(trial / sigma, -ramp_limit, ramp_limit)
        ramp[...] = ramp_new

        def lane_sums(x):
            x = jnp.sum(x, axis=0, keepdims=True)
            out = x[:, 0:128]
            for b in range(1, width // 128):
                out = out + x[:, b * 128:(b + 1) * 128]
            return out

        row_sums = jnp.sum(ext, axis=1, keepdims=True)
        row_sums = jnp.sum(
            jnp.where(diagonal, jnp.broadcast_to(row_sums, (ROWS, 128)), 0.0), axis=0, keepdims=True
        )
        primal_sq = lane_sums((moved - old_levels) ** 2)
        ramp_sq = lane_sums((ramp_new - ramp_now) ** 2)
        report = jnp.where(
            stat_row == 0, row_sums,
            jnp.where(stat_row == 1, primal_sq, jnp.where(stat_row == 2, ramp_sq, 0.0)),
        )

        @pl.when(it == ITERS - 1)
        def _():
            stats[it + 1, me] = report
            stat_start(it + 1)
            for r in range(members):
                rows = slice(r * hour_rows, (r + 1) * hour_rows)
                frag_out[r, 0] = moved[rows, :]
                frag_out[r, 1] = ramp_new[rows, :]
            for r in range(members):
                target = my_group * members + r

                @pl.when(target != me)
                def _():
                    send(
                        frag_out.at[r], frag_in.at[my_chunk], fin_send.at[r], fin_recv.at[my_chunk], target
                    ).start()

                @pl.when(target == me)
                def _():
                    frag_in[my_chunk] = frag_out[r]

        def blocks_of(pair, kind, act):
            for side in range(2):
                for h in range(groups // 2):
                    origin = (pair * 2 + side) * groups + 2 * h + kind

                    @pl.when(origin != me)
                    def _():
                        act(origin)

        def pass_on(origin):
            ext_copy(it, partner, origin, pass_send.at[origin]).wait_recv()
            ext_forward(it, origin).start()

        def take(origin):
            ext_copy(it, partner, origin, pass_send.at[origin]).wait_recv()

        blocks_of(my_pair, core, pass_on)

        @pl.loop(0, pairs)
        def _(j):
            pair = lax.rem(my_pair + j, pairs)

            @pl.when(j < pairs - 1)
            def _():
                blocks_of(lax.rem(my_pair + j + 1, pairs), core, pass_on)

            blocks_of(pair, 1 - core, take)
            lanes = pl.ds(pl.multiple_of(pair * (2 * width), 256), 2 * width)
            x = jnp.concatenate([ext_half[it, pair * 2], ext_half[it, pair * 2 + 1]], axis=1)
            part = lax.dot_general(
                x, masked[:, lanes], (((1,), (1,)), ((), ())), preferred_element_type=f32
            )

            @pl.when(j == 0)
            def _():
                flow_acc[...] = part

            @pl.when(j > 0)
            def _():
                flow_acc[...] += part

        @pl.loop(1, chips)
        def _(d):
            other = lax.rem(chip + d, chips) * 2 + core
            ext_out(it, other).wait_send()
            ext_forward(it, other).wait_send()

        ext_out(it, partner).wait_send()

        old_dual = out_dual[...]
        trial = old_dual + sigma * flow_acc[...]
        bound = limit[...]
        dual_new = trial - sigma * jnp.clip(trial / sigma, base[...] - bound, base[...] + bound)
        out_dual[...] = dual_new
        dual_half[...] = dual_new.astype(bf16)

        @pl.when(it < ITERS - 1)
        def _():
            moved_sq = jnp.sum((dual_new - old_dual) ** 2, axis=0, keepdims=True)
            flow_sq = moved_sq[:, 0:128]
            for b in range(1, ctgs * lines // 128):
                flow_sq = flow_sq + moved_sq[:, b * 128:(b + 1) * 128]
            stats[it + 1, me] = jnp.where(stat_row == 3, flow_sq, report)
            stat_start(it + 1)

    stat_wait(ITERS)
    absorb(ITERS, step_size * omega[0:1, 0:1])
    out_price[...] = price[...]
    for r in range(members):
        target = my_group * members + r

        @pl.when(target != me)
        def _():
            send(
                frag_out.at[r], frag_in.at[my_chunk], fin_send.at[r], fin_recv.at[my_chunk], target
            ).wait_send()

    for c in range(chunks):
        peer = c * groups + home_group

        @pl.when(peer != me)
        def _():
            send(frag_out.at[0], frag_in.at[c], fin_send.at[0], fin_recv.at[c], peer).wait_recv()

    for c in range(chunks):
        out_levels[:, c * width:(c + 1) * width] = frag_in[c, 0]
        out_ramp[:, c * width:(c + 1) * width] = frag_in[c, 1]


def finish(levels, dual, ramp, price, out_levels, out_dual, out_ramp, out_price):
    lines = out_dual.shape[2]
    out_levels[...] = levels[...]
    out_ramp[...] = ramp[...]
    for k in range(out_dual.shape[1]):
        out_dual[:, k, :] = dual[:, k * lines:(k + 1) * lines]
    hour_rows = out_price.shape[0]
    lane = lax.broadcasted_iota(jnp.int32, (1, 128), 1) - lax.axis_index("ctg") * hour_rows
    for r in range(hour_rows):
        out_price[r] = jnp.sum(jnp.where(lane == r, price[0:1], 0.0))


def body(
    flow_tiles,
    tile_pattern,
    monitored,
    ratings,
    base_flow,
    unit_cost,
    unit_floor,
    unit_span,
    ramp_limit,
    ramp_mask,
    demand,
    start_output,
    start_flow_dual,
    start_ramp_dual,
):
    f32, bf16 = jnp.float32, jnp.bfloat16
    ctgs, lines, unit_count = flow_tiles.shape
    n = lax.axis_size("ctg")
    hour_rows = start_output.shape[0]
    hours = hour_rows * n
    groups = hours // ROWS
    chunks = n // groups
    members = ROWS // hour_rows
    width = unit_count // chunks
    flat = ctgs * lines
    step_size = 0.5 / (2.0 + math.sqrt(ctgs * n * lines / unit_count))
    balance = 1.0 / math.sqrt(unit_count)

    vmem = pl.BlockSpec(memory_space=pltpu.VMEM)
    sem = pltpu.SemaphoreType.DMA
    out = pl.pallas_call(
        functools.partial(kernel, n, hour_rows, step_size, balance),
        out_shape=(
            jax.ShapeDtypeStruct((hour_rows, unit_count), f32),
            jax.ShapeDtypeStruct((hours, flat), f32),
            jax.ShapeDtypeStruct((hour_rows, unit_count), f32),
            jax.ShapeDtypeStruct((8, 128), f32),
        ),
        in_specs=[pl.BlockSpec(memory_space=pl.ANY)]
        + [vmem] * 8
        + [pl.BlockSpec(memory_space=pltpu.SMEM)]
        + [vmem] * 4,
        out_specs=(vmem,) * 4,
        scratch_shapes=[
            pltpu.VMEM((flat, unit_count), bf16),
            pltpu.VMEM((hours, flat), f32),
            pltpu.VMEM((3, hour_rows, unit_count), f32),
            pltpu.VMEM((1, flat), f32),
            pltpu.VMEM((hours, flat), bf16),
            pltpu.VMEM((hours, flat), f32),
            pltpu.VMEM((members, 3, hour_rows, width), f32),
            pltpu.VMEM((chunks, 2, hour_rows, width), f32),
            pltpu.VMEM((members, 2, hour_rows, width), f32),
            pltpu.VMEM((ROWS, width), f32),
            pltpu.VMEM((ROWS, width), f32),
            pltpu.VMEM((ROWS, width), f32),
            pltpu.VMEM((ROWS, width), f32),
            pltpu.VMEM((ITERS, 8, width), f32),
            pltpu.VMEM((ITERS, 8, width), f32),
            pltpu.VMEM((chunks, hours, width), bf16),
            pltpu.VMEM((ITERS, chunks, hours, width), bf16),
            pltpu.VMEM((chunks, hours, width), bf16),
            pltpu.VMEM((ITERS, n // 2, ROWS, width), bf16),
            pltpu.VMEM((ITERS, chunks, hours, width), bf16),
            pltpu.VMEM((ITERS + 1, n, 8, 128), f32),
            pltpu.VMEM((8, 128), f32),
            pltpu.VMEM((8, 128), f32),
            sem((ctgs,)),
            sem((chunks,)), sem((members,)), sem((members,)), sem((chunks,)),
            sem((n,)), sem((n,)), sem((n,)), sem((n // 2,)), sem((n,)), sem((n,)), sem((n,)),
            sem((2, n)), sem((2, n)),
            sem((4,)),
        ],
        compiler_params=pltpu.CompilerParams(collective_id=0, has_side_effects=True),
    )(
        flow_tiles,
        tile_pattern,
        monitored,
        ratings.reshape(-1, 128),
        base_flow,
        start_flow_dual,
        start_output,
        unit_cost,
        start_ramp_dual,
        demand,
        unit_floor[None],
        unit_span[None],
        ramp_limit[None],
        ramp_mask[None],
    )
    return pl.pallas_call(
        finish,
        out_shape=(
            jax.ShapeDtypeStruct((hour_rows, unit_count), f32),
            jax.ShapeDtypeStruct((hours, ctgs, lines), f32),
            jax.ShapeDtypeStruct((hour_rows, unit_count), f32),
            jax.ShapeDtypeStruct((hour_rows,), f32),
        ),
        in_specs=[vmem] * 4,
        out_specs=(vmem,) * 3 + (pl.BlockSpec(memory_space=pltpu.SMEM),),
    )(*out)


def solution(mesh):
    return jax.shard_map(
        body,
        mesh=mesh,
        in_specs=(
            P("ctg", None, None),
            P("ctg", None, None),
            P("ctg", None),
            P(),
            P("grp", "ctg", None),
            P(("grp", "ctg"), None),
            P(),
            P(),
            P(),
            P(),
            P(("grp", "ctg")),
            P(("grp", "ctg"), None),
            P("grp", "ctg", None),
            P(("grp", "ctg"), None),
        ),
        out_specs=(
            P(("grp", "ctg"), None),
            P("grp", "ctg", None),
            P(("grp", "ctg"), None),
            P(("grp", "ctg")),
        ),
        check_vma=False,
    )
```

```python
import functools
import math

import jax
import jax.numpy as jnp
from jax import lax
from jax.experimental import pallas as pl
from jax.experimental.pallas import tpu as pltpu
from jax.sharding import PartitionSpec as P

ITERS = 4
ROWS = 16


def send(src, dst, send_sem, recv_sem, target):
    return pltpu.make_async_remote_copy(
        src_ref=src,
        dst_ref=dst,
        send_sem=send_sem,
        recv_sem=recv_sem,
        device_id={"ctg": target},
        device_id_type=pl.DeviceIdType.MESH,
    )


def kernel(
    n, hour_rows, step_size, balance,
    tiles, pattern, index, table, base_in, dual_in, level_in, cost_in, ramp_in, demand,
    floor_in, span_in, ramp_limit_in, ramp_mask_in,
    out_levels, out_dual, out_ramp, out_price,
    masked, base, starts, limit, dual_half, flow_acc,
    start_stage, frag_in, frag_out,
    cost, levels, ramp, extended, halo_ext, halo_ramp,
    pull_out, pair_in, pull_sum, pull_in, ext_half, stats, price, omega,
    tile_sem, frag_send, frag_recv, fin_send, fin_recv,
    pair_send, pair_recv, pull_send, pull_recv, ext_send, ext_recv, pass_send, stat_send, stat_recv,
    halo_sems,
):
    f32 = jnp.float32
    bf16 = jnp.bfloat16
    members = ROWS // hour_rows
    groups = n // members
    chunks = n // groups
    unit_count = tiles.shape[2]
    width = unit_count // chunks
    ctgs, lines = tiles.shape[0], tiles.shape[1]
    hours = groups * ROWS
    pairs = chunks // 2

    me = lax.axis_index("ctg")
    my_chunk = lax.div(me, groups)
    my_group = lax.rem(me, groups)
    home_group = lax.div(me, members)
    home_row = lax.rem(me, members)
    my_pair = lax.div(my_chunk, 2)
    core = lax.rem(me, 2)
    chip = lax.div(me, 2)
    partner = me + 1 - 2 * core
    chips = n // 2
    my_rows = pl.ds(pl.multiple_of(my_group * ROWS, ROWS), ROWS)
    my_lanes = pl.ds(pl.multiple_of(my_chunk * width, 128), width)

    def tile_copy(k):
        return pltpu.make_async_copy(
            tiles.at[k], masked.at[pl.ds(pl.multiple_of(k * lines, lines), lines)], tile_sem.at[k]
        )

    for k in range(ctgs):
        tile_copy(k).start()

    barrier = pltpu.get_barrier_semaphore()

    @pl.loop(1, n)
    def _(d):
        pl.semaphore_signal(
            barrier, inc=1, device_id={"ctg": lax.rem(me + d, n)}, device_id_type=pl.DeviceIdType.MESH
        )

    row_iota = lax.broadcasted_iota(jnp.int32, (128, lines), 0)
    values = table[...].T
    part_a = values.astype(bf16)
    rest = values - part_a.astype(f32)
    part_b = rest.astype(bf16)
    part_c = (rest - part_b.astype(f32)).astype(bf16)
    for k in range(ctgs):
        which = index[k:k + 1, :]
        high = lax.shift_right_logical(which, 7)
        low = lax.bitwise_and(which, 127)
        blocks = table.shape[0] // 128
        got = jnp.zeros((128, lines), f32)
        for b in range(blocks):
            pick = jnp.where(row_iota + b * 128 == high, 1.0, 0.0).astype(bf16)
            for part in (part_a, part_b, part_c):
                got = got + jnp.dot(part[:, b * 128:(b + 1) * 128], pick, preferred_element_type=f32)
        limit[:, k * lines:(k + 1) * lines] = jnp.sum(
            jnp.where(row_iota == low, got, 0.0), axis=0, keepdims=True
        )

    for k in range(ctgs):
        lanes = slice(k * lines, (k + 1) * lines)
        base[:, lanes] = base_in[:, k, :]
        dual = dual_in[:, k, :]
        out_dual[:, lanes] = dual
        dual_half[:, lanes] = dual.astype(bf16)
    omega[...] = jnp.ones_like(omega)
    price[...] = jnp.zeros_like(price)

    pl.semaphore_wait(barrier, n - 1)

    def frag_copy(c, target):
        return send(
            starts.at[:, :, pl.ds(pl.multiple_of(c * width, 128), width)],
            start_stage.at[home_row], frag_send.at[c], frag_recv.at[home_row], target,
        )

    starts[0] = level_in[...]
    starts[1] = cost_in[...]
    starts[2] = ramp_in[...]
    for c in range(chunks):
        target = c * groups + home_group

        @pl.when(target != me)
        def _():
            frag_copy(c, target).start()

        @pl.when(target == me)
        def _():
            start_stage[home_row] = starts[:, :, c * width:(c + 1) * width]

    def stat_copy(slot, target, sender):
        return send(
            stats.at[slot, sender], stats.at[slot, sender],
            stat_send.at[slot % 2, target], stat_recv.at[slot % 2, sender], target,
        )

    def stat_start(slot):
        @pl.loop(1, n)
        def _(d):
            stat_copy(slot, lax.rem(me + d, n), me).start()

    def stat_wait(slot):
        @pl.loop(1, n)
        def _(d):
            peer = lax.rem(me + d, n)
            stat_copy(slot, peer, me).wait_send()
            stat_copy(slot, peer, peer).wait_recv()

    hour = lax.broadcasted_iota(jnp.int32, (4, 128), 1) - me * hour_rows
    own_demand = jnp.zeros((4, 128), f32)
    for r in range(hour_rows):
        own_demand = jnp.where(hour == r, demand[r], own_demand)
    stats[0, me] = own_demand
    stat_start(0)

    tile_count = unit_count // 128
    tile_row = lax.broadcasted_iota(jnp.int32, (tile_count, unit_count), 0)
    tile_lane = lax.broadcasted_iota(jnp.int32, (tile_count, unit_count), 1)
    spread = jnp.where(lax.shift_right_logical(tile_lane, 7) == tile_row, 1.0, 0.0)

    @pl.loop(0, ctgs)
    def _(k):
        tile_copy(k).wait()
        gates = jnp.dot(pattern[k].astype(f32), spread, preferred_element_type=f32)
        for half in range(lines // 128):
            gate = jnp.broadcast_to(gates[half:half + 1], (16, unit_count)).astype(bf16)
            for r in range(8):
                where = pl.ds(pl.multiple_of(k * lines + half * 128 + r * 16, 16), 16)
                masked[where, :] = masked[where, :] * gate

    for r in range(members):
        peer = my_group * members + r

        @pl.when(peer != me)
        def _():
            send(
                starts.at[:, :, pl.ds(0, width)], start_stage.at[r],
                frag_send.at[0], frag_recv.at[r], peer,
            ).wait_recv()

    for c in range(chunks):
        target = c * groups + home_group

        @pl.when(target != me)
        def _():
            frag_copy(c, target).wait_send()

    for r in range(members):
        rows = slice(r * hour_rows, (r + 1) * hour_rows)
        levels[rows, :] = start_stage[r, 0]
        cost[rows, :] = start_stage[r, 1]
        ramp[rows, :] = start_stage[r, 2]

    floor = floor_in[:, my_lanes]
    ceiling = floor + span_in[:, my_lanes]
    ramp_limit = ramp_limit_in[:, my_lanes]
    ramp_on = ramp_mask_in[:, my_lanes].astype(f32)
    block_row = lax.broadcasted_iota(jnp.int32, (ROWS, width), 0)
    lane_here = lax.broadcasted_iota(jnp.int32, (ROWS, 128), 1)
    row_here = lax.broadcasted_iota(jnp.int32, (ROWS, 128), 0) + my_group * ROWS
    diagonal = lane_here == row_here
    hour_lanes = lax.broadcasted_iota(jnp.int32, (1, 128), 1) < hours
    stat_row = lax.broadcasted_iota(jnp.int32, (4, 128), 0)

    ahead = 1 - lax.div(my_pair, pairs // 2)

    def flip(place, length):
        return ahead * (length - 1 - place) + (1 - ahead) * place

    def skip(place, own, length):
        return place + lax.div(place + length - own, length)

    def far_pair(j):
        last = lax.div(j + 1, pairs)
        place = flip(skip(j, flip(my_pair, pairs), pairs), pairs)
        return last * my_pair + (1 - last) * place

    def near_pair(j):
        return far_pair(pairs - 1 - j)

    def far_chip(d):
        return flip(skip(d - 1, flip(chip, chips), chips), chips)

    def block_rows(g):
        return pl.ds(pl.multiple_of(g * ROWS, ROWS), ROWS)

    def pair_copy(it, owner):
        c, g = lax.div(owner, groups), lax.rem(owner, groups)
        return send(
            pull_out.at[c, block_rows(g)], pair_in.at[it, c, block_rows(g)],
            pair_send.at[owner], pair_recv.at[owner], partner,
        )

    def pull_copy(it, target, sender_chip):
        c, g = lax.div(target, groups), lax.rem(target, groups)
        return send(
            pull_sum.at[c, block_rows(g)], pull_in.at[it, sender_chip],
            pull_send.at[target], pull_recv.at[sender_chip], target,
        )

    def ext_copy(it, target, origin, send_sem):
        c, g = lax.div(origin, groups), lax.rem(origin, groups)
        spot = ext_half.at[it, c, block_rows(g)]
        return send(spot, spot, send_sem, ext_recv.at[origin], target)

    def ext_out(it, target):
        return ext_copy(it, target, me, ext_send.at[target])

    def ext_forward(it, origin):
        return ext_copy(it, partner, origin, pass_send.at[origin])

    def halo_ext_copy(it, target):
        return send(extended.at[pl.ds(0, 8)], halo_ext.at[it], halo_sems.at[0], halo_sems.at[1], target)

    def halo_ramp_copy(it, target):
        return send(ramp.at[pl.ds(ROWS - 8, 8)], halo_ramp.at[it], halo_sems.at[2], halo_sems.at[3], target)

    def absorb(slot, sigma):
        total = stats[slot, 0]
        for q in range(1, n):
            total = total + stats[slot, q]
        move = sigma * (balance * (total[0:1] - price[1:2]))
        move = jnp.where(hour_lanes, move, 0.0)
        price[0:1] = price[0:1] + move
        return total, jnp.sum(move * move, axis=1, keepdims=True)

    @pl.loop(0, ITERS)
    def _(it):
        @pl.when(my_group < groups - 1)
        def _():
            halo_ramp_copy(it, me + 1).start()

        @pl.loop(0, pairs + 1)
        def _(j):
            @pl.when(j < pairs)
            def _():
                pair = far_pair(j)
                lanes = pl.ds(pl.multiple_of(pair * (2 * width), 256), 2 * width)
                part = jnp.dot(dual_half[...], masked[:, lanes], preferred_element_type=f32).astype(bf16)
                for side in range(2):
                    c = pair * 2 + side
                    pull_out[c] = part[:, side * width:(side + 1) * width]
                    for h in range(groups // 2):
                        pair_copy(it, c * groups + 2 * h + 1 - core).start()

            @pl.when(j > 0)
            def _():
                pair = far_pair(j - 1)
                for side in range(2):
                    c = pair * 2 + side
                    for h in range(groups // 2):
                        g = 2 * h + core
                        target = c * groups + g
                        pair_copy(it, target).wait_recv()
                        both = (
                            pull_out[c, block_rows(g), :].astype(f32)
                            + pair_in[it, c, block_rows(g), :].astype(f32)
                        ).astype(bf16)

                        @pl.when(target != me)
                        def _():
                            pull_sum[c, block_rows(g), :] = both
                            pull_copy(it, target, chip).start()

                        @pl.when(target == me)
                        def _():
                            pull_in[it, chip] = both

        stat_wait(it)

        @pl.when(it == 0)
        def _():
            first = stats[0, 0]
            for q in range(1, n):
                first = first + stats[0, q]
            price[1:2] = first[0:1]

        @pl.when(it > 0)
        def _():
            old = omega[0:1, 0:1]
            total, price_sq = absorb(it, step_size * old)
            sums = jnp.sum(total, axis=1, keepdims=True)
            dual_sq = sums[3:4] + sums[2:3] + price_sq
            ratio = (dual_sq + 1e-06) / (sums[1:2] + 1e-06)
            omega[...] = jnp.broadcast_to(jnp.sqrt(old) * jnp.sqrt(jnp.sqrt(ratio)), omega.shape)

        weight = omega[0:1, 0:1]
        tau = step_size / weight
        sigma = step_size * weight

        @pl.loop(1, chips)
        def _(d):
            other = lax.rem(chip + d, chips)
            pull_copy(it, other * 2 + core, chip).wait_send()
            pull_copy(it, other * 2 + core, other).wait_recv()

        @pl.loop(0, chips)
        def _(q):
            pair_copy(it, q * 2 + 1 - core).wait_send()

        pulled = pull_in[it, 0].astype(f32)
        for q in range(1, chips):
            pulled = pulled + pull_in[it, q].astype(f32)

        @pl.when(my_group < groups - 1)
        def _():
            halo_ramp_copy(it, me + 1).wait_send()

        @pl.when(my_group > 0)
        def _():
            halo_ramp_copy(it, me - 1).wait_recv()

        @pl.when(my_group == 0)
        def _():
            halo_ramp[it] = jnp.zeros_like(halo_ramp[it])

        ramp_now = ramp[...]
        before = jnp.where(block_row == 0, halo_ramp[it][7:8], pltpu.roll(ramp_now, 1, 0))
        price_here = jnp.sum(
            jnp.where(diagonal, jnp.broadcast_to(price[0:1], (ROWS, 128)), 0.0), axis=1, keepdims=True
        )
        gradient = cost[...] + pulled + ramp_on * (before - ramp_now) + balance * price_here
        old_levels = levels[...]
        moved = jnp.clip(old_levels - tau * gradient, floor, ceiling)
        ext = 2.0 * moved - old_levels
        levels[...] = moved
        ext_half[it, my_chunk, my_rows, :] = ext.astype(bf16)
        extended[...] = ext

        @pl.loop(1, chips)
        def _(d):
            ext_out(it, far_chip(d) * 2 + core).start()

        ext_out(it, partner).start()

        @pl.when(my_group > 0)
        def _():
            halo_ext_copy(it, me - 1).start()
            halo_ext_copy(it, me - 1).wait_send()

        @pl.when(my_group < groups - 1)
        def _():
            halo_ext_copy(it, me + 1).wait_recv()

        @pl.when(my_group == groups - 1)
        def _():
            halo_ext[it] = jnp.zeros_like(halo_ext[it])

        after = jnp.where(block_row == ROWS - 1, halo_ext[it][0:1], pltpu.roll(ext, ROWS - 1, 0))
        change = ramp_on * (after - ext)
        last_hour = block_row + my_group * ROWS == hours - 1
        change = jnp.where(last_hour, 0.0, change)
        trial = ramp_now + sigma * change
        ramp_new = trial - sigma * jnp.clip(trial / sigma, -ramp_limit, ramp_limit)
        ramp[...] = ramp_new

        def lane_sums(x):
            x = jnp.sum(x, axis=0, keepdims=True)
            out = x[:, 0:128]
            for b in range(1, width // 128):
                out = out + x[:, b * 128:(b + 1) * 128]
            return out

        row_sums = jnp.sum(ext, axis=1, keepdims=True)
        row_sums = jnp.sum(
            jnp.where(diagonal, jnp.broadcast_to(row_sums, (ROWS, 128)), 0.0), axis=0, keepdims=True
        )
        primal_sq = lane_sums((moved - old_levels) ** 2)
        ramp_sq = lane_sums((ramp_new - ramp_now) ** 2)
        report = jnp.where(
            stat_row == 0, row_sums,
            jnp.where(stat_row == 1, primal_sq, jnp.where(stat_row == 2, ramp_sq, 0.0)),
        )

        @pl.when(it == ITERS - 1)
        def _():
            stats[it + 1, me] = report
            stat_start(it + 1)
            for r in range(members):
                rows = slice(r * hour_rows, (r + 1) * hour_rows)
                frag_out[r, 0] = moved[rows, :]
                frag_out[r, 1] = ramp_new[rows, :]
            for r in range(members):
                target = my_group * members + r

                @pl.when(target != me)
                def _():
                    send(
                        frag_out.at[r], frag_in.at[my_chunk], fin_send.at[r], fin_recv.at[my_chunk], target
                    ).start()

                @pl.when(target == me)
                def _():
                    frag_in[my_chunk] = frag_out[r]

        def blocks_of(pair, kind, act):
            for side in range(2):
                for h in range(groups // 2):
                    origin = (pair * 2 + side) * groups + 2 * h + kind

                    @pl.when(origin != me)
                    def _():
                        act(origin)

        def pass_on(origin):
            ext_copy(it, partner, origin, pass_send.at[origin]).wait_recv()
            ext_forward(it, origin).start()

        def take(origin):
            ext_copy(it, partner, origin, pass_send.at[origin]).wait_recv()

        blocks_of(my_pair, core, pass_on)

        @pl.loop(0, pairs)
        def _(j):
            pair = near_pair(j)

            @pl.when(j < pairs - 1)
            def _():
                blocks_of(near_pair(j + 1), core, pass_on)

            blocks_of(pair, 1 - core, take)
            lanes = pl.ds(pl.multiple_of(pair * (2 * width), 256), 2 * width)
            x = jnp.concatenate([ext_half[it, pair * 2], ext_half[it, pair * 2 + 1]], axis=1)
            part = lax.dot_general(
                x, masked[:, lanes], (((1,), (1,)), ((), ())), preferred_element_type=f32
            )

            @pl.when(j == 0)
            def _():
                flow_acc[...] = part

            @pl.when(j > 0)
            def _():
                flow_acc[...] += part

        @pl.loop(1, chips)
        def _(d):
            other = lax.rem(chip + d, chips) * 2 + core
            ext_out(it, other).wait_send()
            ext_forward(it, other).wait_send()

        ext_out(it, partner).wait_send()

        old_dual = out_dual[...]
        trial = old_dual + sigma * flow_acc[...]
        bound = limit[...]
        dual_new = trial - sigma * jnp.clip(trial / sigma, base[...] - bound, base[...] + bound)
        out_dual[...] = dual_new
        dual_half[...] = dual_new.astype(bf16)

        @pl.when(it < ITERS - 1)
        def _():
            moved_sq = jnp.sum((dual_new - old_dual) ** 2, axis=0, keepdims=True)
            flow_sq = moved_sq[:, 0:128]
            for b in range(1, ctgs * lines // 128):
                flow_sq = flow_sq + moved_sq[:, b * 128:(b + 1) * 128]
            stats[it + 1, me] = jnp.where(stat_row == 3, flow_sq, report)
            stat_start(it + 1)

    stat_wait(ITERS)
    absorb(ITERS, step_size * omega[0:1, 0:1])
    out_price[...] = price[...]
    for r in range(members):
        target = my_group * members + r

        @pl.when(target != me)
        def _():
            send(
                frag_out.at[r], frag_in.at[my_chunk], fin_send.at[r], fin_recv.at[my_chunk], target
            ).wait_send()

    for c in range(chunks):
        peer = c * groups + home_group

        @pl.when(peer != me)
        def _():
            send(frag_out.at[0], frag_in.at[c], fin_send.at[0], fin_recv.at[c], peer).wait_recv()

    for c in range(chunks):
        out_levels[:, c * width:(c + 1) * width] = frag_in[c, 0]
        out_ramp[:, c * width:(c + 1) * width] = frag_in[c, 1]


def finish(levels, dual, ramp, price, out_levels, out_dual, out_ramp, out_price):
    lines = out_dual.shape[2]
    out_levels[...] = levels[...]
    out_ramp[...] = ramp[...]
    for k in range(out_dual.shape[1]):
        out_dual[:, k, :] = dual[:, k * lines:(k + 1) * lines]
    hour_rows = out_price.shape[0]
    lane = lax.broadcasted_iota(jnp.int32, (1, 128), 1) - lax.axis_index("ctg") * hour_rows
    for r in range(hour_rows):
        out_price[r] = jnp.sum(jnp.where(lane == r, price[0:1], 0.0))


def body(
    flow_tiles,
    tile_pattern,
    monitored,
    ratings,
    base_flow,
    unit_cost,
    unit_floor,
    unit_span,
    ramp_limit,
    ramp_mask,
    demand,
    start_output,
    start_flow_dual,
    start_ramp_dual,
):
    f32, bf16 = jnp.float32, jnp.bfloat16
    ctgs, lines, unit_count = flow_tiles.shape
    n = lax.axis_size("ctg")
    hour_rows = start_output.shape[0]
    hours = hour_rows * n
    groups = hours // ROWS
    chunks = n // groups
    members = ROWS // hour_rows
    width = unit_count // chunks
    flat = ctgs * lines
    step_size = 0.5 / (2.0 + math.sqrt(ctgs * n * lines / unit_count))
    balance = 1.0 / math.sqrt(unit_count)

    vmem = pl.BlockSpec(memory_space=pltpu.VMEM)
    sem = pltpu.SemaphoreType.DMA
    out = pl.pallas_call(
        functools.partial(kernel, n, hour_rows, step_size, balance),
        out_shape=(
            jax.ShapeDtypeStruct((hour_rows, unit_count), f32),
            jax.ShapeDtypeStruct((hours, flat), f32),
            jax.ShapeDtypeStruct((hour_rows, unit_count), f32),
            jax.ShapeDtypeStruct((8, 128), f32),
        ),
        in_specs=[pl.BlockSpec(memory_space=pl.ANY)]
        + [vmem] * 8
        + [pl.BlockSpec(memory_space=pltpu.SMEM)]
        + [vmem] * 4,
        out_specs=(vmem,) * 4,
        scratch_shapes=[
            pltpu.VMEM((flat, unit_count), bf16),
            pltpu.VMEM((hours, flat), f32),
            pltpu.VMEM((3, hour_rows, unit_count), f32),
            pltpu.VMEM((1, flat), f32),
            pltpu.VMEM((hours, flat), bf16),
            pltpu.VMEM((hours, flat), f32),
            pltpu.VMEM((members, 3, hour_rows, width), f32),
            pltpu.VMEM((chunks, 2, hour_rows, width), f32),
            pltpu.VMEM((members, 2, hour_rows, width), f32),
            pltpu.VMEM((ROWS, width), f32),
            pltpu.VMEM((ROWS, width), f32),
            pltpu.VMEM((ROWS, width), f32),
            pltpu.VMEM((ROWS, width), f32),
            pltpu.VMEM((ITERS, 8, width), f32),
            pltpu.VMEM((ITERS, 8, width), f32),
            pltpu.VMEM((chunks, hours, width), bf16),
            pltpu.VMEM((ITERS, chunks, hours, width), bf16),
            pltpu.VMEM((chunks, hours, width), bf16),
            pltpu.VMEM((ITERS, n // 2, ROWS, width), bf16),
            pltpu.VMEM((ITERS, chunks, hours, width), bf16),
            pltpu.VMEM((ITERS + 1, n, 4, 128), f32),
            pltpu.VMEM((8, 128), f32),
            pltpu.VMEM((8, 128), f32),
            sem((ctgs,)),
            sem((chunks,)), sem((members,)), sem((members,)), sem((chunks,)),
            sem((n,)), sem((n,)), sem((n,)), sem((n // 2,)), sem((n,)), sem((n,)), sem((n,)),
            sem((2, n)), sem((2, n)),
            sem((4,)),
        ],
        compiler_params=pltpu.CompilerParams(collective_id=0, has_side_effects=True),
    )(
        flow_tiles,
        tile_pattern,
        monitored,
        ratings.reshape(-1, 128),
        base_flow,
        start_flow_dual,
        start_output,
        unit_cost,
        start_ramp_dual,
        demand,
        unit_floor[None],
        unit_span[None],
        ramp_limit[None],
        ramp_mask[None],
    )
    return pl.pallas_call(
        finish,
        out_shape=(
            jax.ShapeDtypeStruct((hour_rows, unit_count), f32),
            jax.ShapeDtypeStruct((hours, ctgs, lines), f32),
            jax.ShapeDtypeStruct((hour_rows, unit_count), f32),
            jax.ShapeDtypeStruct((hour_rows,), f32),
        ),
        in_specs=[vmem] * 4,
        out_specs=(vmem,) * 3 + (pl.BlockSpec(memory_space=pltpu.SMEM),),
    )(*out)


def solution(mesh):
    return jax.shard_map(
        body,
        mesh=mesh,
        in_specs=(
            P("ctg", None, None),
            P("ctg", None, None),
            P("ctg", None),
            P(),
            P("grp", "ctg", None),
            P(("grp", "ctg"), None),
            P(),
            P(),
            P(),
            P(),
            P(("grp", "ctg")),
            P(("grp", "ctg"), None),
            P("grp", "ctg", None),
            P(("grp", "ctg"), None),
        ),
        out_specs=(
            P(("grp", "ctg"), None),
            P("grp", "ctg", None),
            P(("grp", "ctg"), None),
            P(("grp", "ctg")),
        ),
        check_vma=False,
    )
```
